256 devices in a mesh: depth: 256 (over x, y, z, core).
Axes of the slice: x: 4, y: 4, z: 8, core: 2. Of those that a mesh axis runs over, the one named last changes fastest.
Arguments:
- w_in: bfloat16 [512, 512, 1024], P('depth'), may hold values from -0.25 to 0.25
- w_out: bfloat16 [512, 1024, 512], P('depth'), may hold values from -0.0234375 to 0.0234375
- checkpoint: bfloat16 [256, 256, 512], P('depth'), may hold values from -6 to 6
- guess: float32 [256, 256, 512], P('depth'), may hold values from -6 to 6
- terminal: float32 [256, 512], replicated, may hold values from -6 to 6
Outputs:
- adjoint: float32 [512, 256, 512], P('depth')
- grad_in: bfloat16 [512, 512, 1024], P('depth')
- grad_out: bfloat16 [512, 1024, 512], P('depth')
The draws below stay inside these ranges and needn't reach their ends.
All inputs are finite; a program needn't handle non-finite values.
Results may differ from the reference program's by a relative error of at most 0.017.
Values sent between devices are 32-bit elements; how exact they have to be, the bound alone decides.
A program may use at most 64 MiB of HBM per device.

```python
import jax
import jax.numpy as jnp
from jax import lax

D = 512
FF = 1024
ROWS = 256
LEVELS = 4
LAYERS = 512


def steps_of(own_key, shape, cuts, least, top_value):
    def one(position, blocks):
        draws = jax.random.uniform(jax.random.fold_in(jax.random.fold_in(own_key, 6), position), (blocks,), jnp.float32, least / len(cuts), top_value / len(cuts))
        return jnp.repeat(jnp.exp(draws), shape[position] // blocks).reshape((-1,) + (1,) * (len(shape) - position - 1))

    level = one(*cuts[0])
    for cut in cuts[1:]:
        level = level * one(*cut)
    return level


def bell_draw(own_key, shape, deviation, most, pieces=(), kind=jnp.bfloat16):
    level = steps_of(own_key, shape, pieces, -0.22, 0.18) if pieces else 1.0
    drawn = jax.random.normal(own_key, shape, jnp.float32) * deviation * level
    return jnp.minimum(jnp.maximum(drawn, -most), most).astype(kind)


def setup_inputs(seed: int = 0) -> dict:
    streams_of = jax.random.split(jax.random.key(seed), 6)
    return {
        "w_in": bell_draw(streams_of[0], (LAYERS, D, FF), D ** -0.5, 0.25, ((0, 256),)),
        "w_out": bell_draw(streams_of[1], (LAYERS, FF, D), (64 * FF) ** -0.5, 0.0234375, ((0, 256),)),
        "checkpoint": bell_draw(streams_of[2], (LAYERS // 2, ROWS, D), 1.0, 6.0, ((0, 256),)),
        "guess": bell_draw(streams_of[3], (LAYERS // 2, ROWS, D), 1.0, 6.0, ((0, 256),), jnp.float32),
        "terminal": bell_draw(streams_of[4], (ROWS, D), 1.0, 6.0, (), jnp.float32),
    }


def tangent_of(vector, w_second, slope):
    product = jnp.dot(vector.astype(jnp.bfloat16), w_second.T, preferred_element_type=jnp.float32)
    return (product * slope).astype(jnp.bfloat16)


def forward(checkpoint, w_in, w_out):
    def one(items):
        start, first_pair, second_pair = items
        h_zero = jnp.tanh(jnp.dot(start, first_pair[0], preferred_element_type=jnp.float32))
        act_zero = h_zero.astype(jnp.bfloat16)
        upper = start.astype(jnp.float32) + jnp.dot(act_zero, second_pair[0], preferred_element_type=jnp.float32)
        upper_b = upper.astype(jnp.bfloat16)
        h_one = jnp.tanh(jnp.dot(upper_b, first_pair[1], preferred_element_type=jnp.float32))
        states = jnp.stack([start, upper_b])
        acts = jnp.stack([act_zero, h_one.astype(jnp.bfloat16)])
        slopes = jnp.stack([1.0 - h_zero * h_zero, 1.0 - h_one * h_one])
        return states, acts, slopes

    states, acts, slopes = lax.map(one, (checkpoint, w_in.reshape(-1, 2, D, FF), w_out.reshape(-1, 2, FF, D)))
    return states.reshape(LAYERS, ROWS, D), acts.reshape(LAYERS, ROWS, FF), slopes.reshape(LAYERS, ROWS, FF)


def propagate(points, layers, factor, w_in, w_out, slopes):
    def one(items):
        vector, layer = items
        w_first = lax.dynamic_index_in_dim(w_in, layer, 0, False)
        w_second = lax.dynamic_index_in_dim(w_out, layer, 0, False)
        slope = lax.dynamic_index_in_dim(slopes, layer, 0, False)
        tangent = tangent_of(vector, w_second, slope)
        return vector + factor * jnp.dot(tangent, w_first.T, preferred_element_type=jnp.float32)

    return lax.map(one, (points, layers))


def cycle(level, values, rhs, fixed, w_in, w_out, slopes):
    half = values.shape[0] // 2
    stride = 2 ** level
    factor = float(stride)
    odd_layers = ((2 * jnp.arange(half) + 1) * stride).astype(jnp.int32)
    even_layers = (2 * jnp.arange(half) * stride).astype(jnp.int32)

    def relax_f(values):
        nxt = jnp.concatenate([values[2::2], fixed[None]], 0)
        return values.at[1::2].set(propagate(nxt, odd_layers, factor, w_in, w_out, slopes) + rhs[1::2])

    def relax_c(values):
        return values.at[0::2].set(propagate(values[1::2], even_layers, factor, w_in, w_out, slopes) + rhs[0::2])

    values = relax_f(values)
    if level > 0:
        values = relax_c(values)
        values = relax_f(values)
    if level == LEVELS - 1:
        return values
    resid = propagate(values[1::2], even_layers, factor, w_in, w_out, slopes) + rhs[0::2] - values[0::2]
    correction = cycle(level + 1, jnp.zeros_like(resid), resid, jnp.zeros_like(fixed), w_in, w_out, slopes)
    values = values.at[0::2].add(correction)
    return relax_f(values)


def reference(w_in, w_out, checkpoint, guess, terminal):
    states, acts, slopes = forward(checkpoint, w_in, w_out)
    start = jnp.zeros((LAYERS, ROWS, D), jnp.float32).at[0::2].set(guess)
    adjoint = cycle(0, start, jnp.zeros((LAYERS, ROWS, D), jnp.float32), terminal, w_in, w_out, slopes)
    nexts = jnp.concatenate([adjoint[1:], terminal[None]], 0)

    def grads(items):
        w_second, slope, state, act, nxt = items
        tangent = tangent_of(nxt, w_second, slope)
        first = jnp.dot(state.T, tangent, preferred_element_type=jnp.float32).astype(jnp.bfloat16)
        second = jnp.dot(act.T, nxt.astype(jnp.bfloat16), preferred_element_type=jnp.float32).astype(jnp.bfloat16)
        return first, second

    grad_in, grad_out = lax.map(grads, (w_out, slopes, states, acts, nexts))
    return adjoint, grad_in, grad_out
```

```python
import functools

import jax
import jax.numpy as jnp
from jax import lax
from jax.experimental import pallas as pl
from jax.experimental.pallas import tpu as pltpu
from jax.sharding import PartitionSpec as P

MESH = pl.DeviceIdType.MESH
BF = jnp.bfloat16
F32 = jnp.float32

GUESS_IN, GUESS, R1, VC, Y, R2, WC, U, R3, X, XUP, W_IN, W, E = range(14)
MESSAGES = 14


def matmul(a, b):
    return jnp.dot(a, b, preferred_element_type=F32)


def kernel(
    count, rows_per, wi_h, wo_h, cp_h, gs_h, tm_h, adj_h, gi_h, go_h,
    wi, wo, wit, wot, cp, gs, state_one, act, slope, tang,
    g_next, r1, r1_next, vc, vc_next, y, r2, r2_next, wc, wc_next, u, r3, r3_next, x, x_next, x_up, w, w_next, w_above,
    e_next, adj, gi, go, load_sem, store_sem, send_sem, recv_sem,
):
    n = lax.axis_index("depth")
    core = lax.rem(n, 2)
    even = core == 0
    chip_odd = lax.rem(n, 4) == 2
    chip_even = lax.rem(n, 4) == 0
    pair_odd = lax.rem(n, 8) == 4
    pair_even = lax.rem(n, 8) == 0
    total = cp.shape[0]
    chunks = total // rows_per

    def rows_of(k):
        return pl.ds(pl.multiple_of(k * rows_per, rows_per), rows_per)

    def message(kind, k, source, target, peer, receives=None):
        rows = rows_of(k)
        return pltpu.make_async_remote_copy(
            src_ref=source.at[rows],
            dst_ref=target.at[rows],
            send_sem=send_sem.at[kind, k],
            recv_sem=recv_sem.at[kind if receives is None else receives, k],
            device_id=(peer,),
            device_id_type=MESH,
        )

    def arrived(kind, k, target):
        message(kind, k, target, target, n).wait_recv()

    def each(body):
        def step(k, carry):
            body(k, rows_of(k))
            return carry

        lax.fori_loop(0, chunks, step, 0)

    def tangent(value, layer, rows):
        return (matmul(value.astype(BF), wot[layer]) * slope[layer, rows, :]).astype(BF)

    def moved(value, layer, rows):
        return matmul(tangent(value, layer, rows), wit[layer])

    loads = [
        pltpu.make_async_copy(source, target, load_sem.at[place])
        for place, (source, target) in enumerate(
            (
                (cp_h.at[0], cp),
                (wi_h.at[0], wi.at[0]),
                (wo_h.at[0], wo.at[0]),
                (wi_h.at[1], wi.at[1]),
                (wo_h.at[1], wo.at[1]),
                (gs_h.at[0], gs),
            )
        )
    ]
    for copy in loads:
        copy.start()

    barrier = pltpu.get_barrier_semaphore()
    peers = (
        (n + 1, jnp.logical_and(n >= 0, n + 1 < count)),
        (n - 1, n >= 1),
        (n + 2, jnp.logical_and(even, n + 2 < count)),
        (n - 2, jnp.logical_and(even, n >= 2)),
        (n + 4, jnp.logical_and(chip_even, n + 4 < count)),
        (n - 4, jnp.logical_and(chip_even, n >= 4)),
    )
    for peer, there in peers:

        @pl.when(there)
        def _(peer=peer):
            pl.semaphore_signal(barrier, inc=1, device_id=(peer,), device_id_type=MESH)

    greeted = sum(jnp.where(there, 1, 0) for _, there in peers)
    pl.semaphore_wait(barrier, greeted)

    @pl.when(jnp.logical_not(even))
    def _():
        each(lambda k, rows: message(GUESS_IN, k, gs_h.at[0], g_next, n - 1).start())

    @pl.when(jnp.logical_and(even, n >= 1))
    def _():
        each(lambda k, rows: message(GUESS, k, gs_h.at[0], g_next, n - 1).start())

    def terminal_copy(k):
        rows = rows_of(k)
        return pltpu.make_async_copy(tm_h.at[rows], g_next.at[rows], recv_sem.at[GUESS, k])

    @pl.when(n == count - 1)
    def _():
        each(lambda k, rows: terminal_copy(k).start())
        vc_next[...] = jnp.zeros_like(vc_next)

    @pl.when(n == count - 2)
    def _():
        wc_next[...] = jnp.zeros_like(wc_next)
        x_up[...] = jnp.zeros_like(x_up)

    @pl.when(n == count - 4)
    def _():
        x_next[...] = jnp.zeros_like(x_next)

    loads[0].wait()
    loads[1].wait()
    h = jnp.tanh(matmul(cp[...], wi[0]))
    act[0] = h.astype(BF)
    slope[0] = 1.0 - h * h
    loads[2].wait()
    state_one[...] = (cp[...].astype(F32) + matmul(act[0], wo[0])).astype(BF)
    loads[3].wait()
    h = jnp.tanh(matmul(state_one[...], wi[1]))
    act[1] = h.astype(BF)
    slope[1] = 1.0 - h * h
    loads[4].wait()
    for layer in (1, 0):
        wot[layer] = wo[layer].T
        wit[layer] = wi[layer].T
    loads[5].wait()

    @pl.when(even)
    def _core_zero():
        each(lambda k, rows: arrived(GUESS_IN, k, g_next))
        every = pl.ds(0, total)
        value = g_next[...]
        value = value + moved(value, 1, every)
        value = value + moved(value, 0, every)
        r1[...] = value - gs[...]

        def level_one(k, rows):
            arrived(R1, k, r1_next)
            value = r1_next[rows, :]
            vc[rows, :] = value + 2.0 * moved(value, 0, rows) + r1[rows, :]

            @pl.when(n >= 1)
            def _():
                message(VC, k, vc, vc_next, n - 1).start()

        each(level_one)

        def level_one_residual(k, rows):
            arrived(Y, k, y)
            value = y[rows, :]
            r2[rows, :] = value + 2.0 * moved(value, 0, rows)

            @pl.when(chip_odd)
            def _():
                message(R2, k, r2, r2_next, n - 2).start()

        each(level_one_residual)

        @pl.when(chip_even)
        def _even_chip():
            def level_two(k, rows):
                arrived(R2, k, r2_next)
                value = r2_next[rows, :]
                wc[rows, :] = value + 4.0 * moved(value, 0, rows) + r2[rows, :]

                @pl.when(n >= 2)
                def _():
                    message(WC, k, wc, wc_next, n - 2).start()

            each(level_two)

            def level_two_residual(k, rows):
                arrived(U, k, u)
                value = u[rows, :]
                r3[rows, :] = value + 4.0 * moved(value, 0, rows)

                @pl.when(pair_odd)
                def _():
                    message(R3, k, r3, r3_next, n - 4).start()

            each(level_two_residual)

            @pl.when(pair_even)
            def _():
                def level_three(k, rows):
                    arrived(R3, k, r3_next)
                    value = r3_next[rows, :]
                    x[rows, :] = value + 8.0 * moved(value, 0, rows) + r3[rows, :]

                    @pl.when(n >= 4)
                    def _():
                        message(X, k, x, x_next, n - 4).start()

                each(level_three)

                @pl.when(n >= 2)
                def _():
                    each(lambda k, rows: message(XUP, k, x, x_up, n - 2).start())

            @pl.when(pair_odd)
            def _():
                def level_three(k, rows):
                    @pl.when(n + 4 < count)
                    def _():
                        arrived(X, k, x_next)

                    value = x_next[rows, :]
                    x[rows, :] = value + 8.0 * moved(value, 0, rows) + r3[rows, :]
                    message(XUP, k, x, x_up, n - 2).start()

                each(level_three)

            w[...] = wc[...] + x[...]

        @pl.when(chip_odd)
        def _odd_chip():
            def level_two(k, rows):
                @pl.when(n + 2 < count)
                def _():
                    arrived(WC, k, wc_next)

                value = wc_next[rows, :]
                u_out = value + 4.0 * moved(value, 0, rows)
                wc[rows, :] = u_out
                message(U, k, wc, u, n - 2).start()

            each(level_two)

            def level_two_up(k, rows):
                @pl.when(n + 2 < count)
                def _():
                    arrived(XUP, k, x_up)

                value = wc_next[rows, :] + x_up[rows, :]
                w_next[rows, :] = value
                message(W_IN, k, w_next, w_above, n + 1, W).start()
                w[rows, :] = value + 4.0 * moved(value, 0, rows) + r2[rows, :]
                message(W, k, w, w_above, n - 1).start()

            each(level_two_up)

        adj[0] = gs[...] + (vc[...] + w[...])

        def fine(k, rows):
            arrived(E, k, e_next)
            value = e_next[rows, :]
            part = tangent(value, 1, rows)
            tang[1, rows, :] = part
            value = value + matmul(part, wit[1])
            adj[1, rows, :] = value
            tang[0, rows, :] = tangent(value, 0, rows)

        each(fine)

    @pl.when(jnp.logical_not(even))
    def _core_one():
        def fine_residual(k, rows):
            @pl.when(n + 1 < count)
            def _():
                arrived(GUESS, k, g_next)

            @pl.when(n + 1 == count)
            def _():
                terminal_copy(k).wait()

            value = g_next[rows, :]
            value = value + moved(value, 1, rows)
            value = value + moved(value, 0, rows)
            r1[rows, :] = value - gs[rows, :]
            message(R1, k, r1, r1_next, n - 1).start()

        each(fine_residual)

        def level_one(k, rows):
            @pl.when(n + 1 < count)
            def _():
                arrived(VC, k, vc_next)

            value = vc_next[rows, :]
            vc[rows, :] = value + 2.0 * moved(value, 0, rows)
            message(Y, k, vc, y, n - 1).start()

        each(level_one)

        def level_one_up(k, rows):
            arrived(W, k, w_above)
            value = vc_next[rows, :] + w_above[rows, :]
            e_next[rows, :] = g_next[rows, :] + value
            adj[0, rows, :] = gs[rows, :] + (value + 2.0 * moved(value, 0, rows) + r1[rows, :])
            message(E, k, adj.at[0], e_next, n - 1).start()

        each(level_one_up)

        every = pl.ds(0, total)
        value = e_next[...]
        part = tangent(value, 1, every)
        tang[1] = part
        value = value + matmul(part, wit[1])
        adj[1] = value
        tang[0] = tangent(value, 0, every)

    def transposed_dot(a, b):
        return lax.dot_general(a, b, (((0,), (0,)), ((), ())), preferred_element_type=F32)

    stores = [
        pltpu.make_async_copy(source, target, store_sem.at[place])
        for place, (source, target) in enumerate(
            (
                (adj, adj_h),
                (gi.at[1], gi_h.at[1]),
                (go.at[1], go_h.at[1]),
                (gi.at[0], gi_h.at[0]),
                (go.at[0], go_h.at[0]),
            )
        )
    ]
    stores[0].start()
    gi[1] = transposed_dot(state_one[...], tang[1]).astype(BF)
    stores[1].start()
    go[1] = transposed_dot(act[1], e_next[...].astype(BF)).astype(BF)
    stores[2].start()
    gi[0] = transposed_dot(cp[...], tang[0]).astype(BF)
    stores[3].start()
    go[0] = transposed_dot(act[0], adj[1].astype(BF)).astype(BF)
    stores[4].start()

    sent = (
        (GUESS_IN, jnp.logical_not(even)),
        (GUESS, jnp.logical_and(even, n >= 1)),
        (R1, jnp.logical_not(even)),
        (VC, jnp.logical_and(even, n >= 1)),
        (Y, jnp.logical_not(even)),
        (R2, chip_odd),
        (WC, jnp.logical_and(chip_even, n >= 2)),
        (U, chip_odd),
        (R3, pair_odd),
        (X, jnp.logical_and(pair_even, n >= 4)),
        (XUP, jnp.logical_and(chip_even, n >= 2)),
        (W_IN, chip_odd),
        (W, chip_odd),
        (E, jnp.logical_not(even)),
    )
    for kind, done in sent:

        @pl.when(done)
        def _(kind=kind):
            each(lambda k, rows: message(kind, k, r1, r1, n).wait_send())

    for copy in stores:
        copy.wait()


def local(w_in, w_out, checkpoint, guess, terminal, rows_per=32):
    count = lax.axis_size("depth")
    pair, width, hidden = w_in.shape
    rows = terminal.shape[0]
    chunks = rows // rows_per
    anywhere = pl.BlockSpec(memory_space=pl.ANY)
    plane = pltpu.VMEM((rows, width), F32)
    return pl.pallas_call(
        functools.partial(kernel, count, rows_per),
        out_shape=(
            jax.ShapeDtypeStruct((pair, rows, width), F32),
            jax.ShapeDtypeStruct((pair, width, hidden), BF),
            jax.ShapeDtypeStruct((pair, hidden, width), BF),
        ),
        in_specs=[anywhere] * 5,
        out_specs=(anywhere,) * 3,
        scratch_shapes=[
            pltpu.VMEM((pair, width, hidden), BF),
            pltpu.VMEM((pair, hidden, width), BF),
            pltpu.VMEM((pair, hidden, width), BF),
            pltpu.VMEM((pair, width, hidden), BF),
            pltpu.VMEM((rows, width), BF),
            plane,
            pltpu.VMEM((rows, width), BF),
            pltpu.VMEM((pair, rows, hidden), BF),
            pltpu.VMEM((pair, rows, hidden), F32),
            pltpu.VMEM((pair, rows, hidden), BF),
        ]
        + [plane] * 20
        + [
            pltpu.VMEM((pair, rows, width), F32),
            pltpu.VMEM((pair, width, hidden), BF),
            pltpu.VMEM((pair, hidden, width), BF),
            pltpu.SemaphoreType.DMA((6,)),
            pltpu.SemaphoreType.DMA((5,)),
            pltpu.SemaphoreType.DMA((MESSAGES, chunks)),
            pltpu.SemaphoreType.DMA((MESSAGES, chunks)),
        ],
        compiler_params=pltpu.CompilerParams(
            collective_id=0, has_side_effects=True, vmem_limit_bytes=56 << 20
        ),
        name="vcycle",
    )(w_in, w_out, checkpoint, guess, terminal)


def solution(mesh):
    split = P("depth", None, None)
    return jax.shard_map(
        local,
        mesh=mesh,
        in_specs=(split, split, split, split, P()),
        out_specs=(split, split, split),
        check_vma=False,
    )
```

```python
import functools

import jax
import jax.numpy as jnp
from jax import lax
from jax.experimental import pallas as pl
from jax.experimental.pallas import tpu as pltpu
from jax.sharding import PartitionSpec as P

MESH = pl.DeviceIdType.MESH
BF = jnp.bfloat16
F32 = jnp.float32

GUESS_IN, GUESS, R1, VC, R2, WC, U, R3, X, XUP, W, W_DOWN, E = range(13)
MESSAGES = 13
EVEN, ODD, OTHER = 0, 1, 2


def matmul(a, b):
    return jnp.dot(a, b, preferred_element_type=F32)


def kernel(
    count, rows_per, wi_h, wo_h, cp_h, gs_h, tm_h, tang, act, state, nexts, adj,
    wi, wo, wit, wot, wide_in, wide_out, gs, slope,
    g_next, r1, r1_next, vc, vc_next, r2, r2_next, wc, wc_next, u, u_own, r3, r3_next, x, x_next, x_up, w, w_next, w_down, e_next,
    load_sem, hand_send, hand_recv, send_sem, recv_sem,
):
    n = lax.axis_index("depth")
    core_zero = lax.rem(n, 2) == 0
    core_one = lax.rem(n, 2) == 1
    chip_even = lax.rem(n, 4) == 1
    chip_odd = lax.rem(n, 4) == 3
    pair_even = lax.rem(n, 8) == 1
    pair_odd = lax.rem(n, 8) == 5
    total = gs.shape[0]
    chunks = total // rows_per
    every = pl.ds(0, total)

    def rows_of(k, several=1):
        size = rows_per * several
        return pl.ds(pl.multiple_of(k * size, size), size)

    def message(kind, k, source, target, peer):
        rows = rows_of(k)
        return pltpu.make_async_remote_copy(
            src_ref=source.at[rows],
            dst_ref=target.at[rows],
            send_sem=send_sem.at[kind, k],
            recv_sem=recv_sem.at[kind, k],
            device_id=(peer,),
            device_id_type=MESH,
        )

    def arrived(kind, k, target):
        message(kind, k, target, target, n).wait_recv()

    def each(body, several=1):
        def step(k, carry):
            body(k, rows_of(k, several))
            return carry

        lax.fori_loop(0, chunks // several, step, 0)

    def tangent(value, layer, rows):
        return (matmul(value.astype(BF), wot[layer]) * slope[layer, rows, :]).astype(BF)

    def moved(value, layer, rows):
        return matmul(tangent(value, layer, rows), wit[layer])

    loads = [
        pltpu.make_async_copy(source, target, load_sem.at[place])
        for place, (source, target) in enumerate(
            (
                (wo_h.at[0], wo.at[0]),
                (wi_h.at[0], wi.at[0]),
                (cp_h.at[0], state.at[0]),
                (wi_h.at[1], wi.at[1]),
                (wo_h.at[1], wo.at[1]),
                (gs_h.at[0], gs),
            )
        )
    ]
    for copy in loads:
        copy.start()

    barrier = pltpu.get_barrier_semaphore()
    peers = (
        (n + 1, n + 1 < count),
        (n - 1, n >= 1),
        (n + 2, jnp.logical_and(core_one, n + 2 < count)),
        (n - 2, jnp.logical_and(core_one, n >= 2)),
        (n + 4, jnp.logical_and(chip_even, n + 4 < count)),
        (n - 4, jnp.logical_and(chip_even, n >= 4)),
    )
    for peer, there in peers:

        @pl.when(there)
        def _(peer=peer):
            pl.semaphore_signal(barrier, inc=1, device_id=(peer,), device_id_type=MESH)

    greeted = sum(jnp.where(there, 1, 0) for _, there in peers)
    pl.semaphore_wait(barrier, greeted)

    @pl.when(core_one)
    def _():
        each(lambda k, rows: message(GUESS_IN, k, gs_h.at[0], g_next, n - 1).start())

    @pl.when(jnp.logical_and(core_zero, n >= 1))
    def _():
        each(lambda k, rows: message(GUESS, k, gs_h.at[0], g_next, n - 1).start())

    def terminal_copy(k):
        rows = rows_of(k)
        return pltpu.make_async_copy(tm_h.at[rows], g_next.at[rows], recv_sem.at[GUESS, k])

    @pl.when(n == count - 1)
    def _():
        each(lambda k, rows: terminal_copy(k).start())
        vc_next[...] = jnp.zeros_like(vc_next)
        wc_next[...] = jnp.zeros_like(wc_next)
        x_up[...] = jnp.zeros_like(x_up)

    @pl.when(n == count - 3)
    def _():
        x_next[...] = jnp.zeros_like(x_next)

    def handed(place, source, target, peer):
        return pltpu.make_async_remote_copy(
            src_ref=source,
            dst_ref=target,
            send_sem=hand_send.at[place],
            recv_sem=hand_recv.at[place],
            device_id=(peer,),
            device_id_type=MESH,
        )

    def hand_out(peer):
        return handed(0, wide_out, wide_out, peer)

    def hand_in(peer):
        return handed(1, wide_in, wide_in, peer)

    def hand_slope(peer):
        return handed(2, slope.at[EVEN], slope.at[OTHER], peer)

    loads[0].wait()
    wot[EVEN] = wo[EVEN].T

    @pl.when(core_zero)
    def _():
        wide_out[...] = wot[EVEN].astype(F32)
        hand_out(n + 1).start()

    loads[1].wait()
    wit[EVEN] = wi[EVEN].T

    @pl.when(core_zero)
    def _():
        wide_in[...] = wit[EVEN].astype(F32)
        hand_in(n + 1).start()

    loads[2].wait()
    h = jnp.tanh(matmul(state[EVEN], wi[EVEN]))
    act[EVEN] = h.astype(BF)
    slope[EVEN] = 1.0 - h * h

    @pl.when(core_zero)
    def _():
        hand_slope(n + 1).start()

    state[ODD] = (state[EVEN].astype(F32) + matmul(act[EVEN], wo[EVEN])).astype(BF)
    loads[3].wait()
    h = jnp.tanh(matmul(state[ODD], wi[ODD]))
    act[ODD] = h.astype(BF)
    slope[ODD] = 1.0 - h * h
    loads[4].wait()
    wot[ODD] = wo[ODD].T
    wit[ODD] = wi[ODD].T
    loads[5].wait()

    @pl.when(core_zero)
    def _core_zero():
        each(lambda k, rows: arrived(GUESS_IN, k, g_next))
        value = g_next[...]
        value = value + moved(value, ODD, every)
        value = value + moved(value, EVEN, every)
        r1[...] = value - gs[...]

        def level_one(k, rows):
            arrived(R1, k, r1_next)
            value = r1_next[rows, :]
            vc[rows, :] = value + 2.0 * moved(value, EVEN, rows) + r1[rows, :]

            @pl.when(n >= 1)
            def _():
                message(VC, k, vc, vc_next, n - 1).start()

        each(level_one)
        each(lambda k, rows: arrived(W_DOWN, k, w_down))
        adj[EVEN] = gs[...] + (vc[...] + w_down[...])

        def fine(k, rows):
            arrived(E, k, e_next)
            value = e_next[rows, :]
            nexts[ODD, rows, :] = value.astype(BF)
            part = tangent(value, ODD, rows)
            tang[ODD, rows, :] = part
            value = value + matmul(part, wit[ODD])
            adj[ODD, rows, :] = value
            nexts[EVEN, rows, :] = value.astype(BF)
            tang[EVEN, rows, :] = tangent(value, EVEN, rows)

        each(fine)

    @pl.when(core_one)
    def _core_one():
        def fine_residual(pair, rows):
            for k in (2 * pair, 2 * pair + 1):

                @pl.when(n + 1 < count)
                def _(k=k):
                    arrived(GUESS, k, g_next)

                @pl.when(n + 1 == count)
                def _(k=k):
                    terminal_copy(k).wait()

            value = g_next[rows, :]
            value = value + moved(value, ODD, rows)
            value = value + moved(value, EVEN, rows)
            r1[rows, :] = value - gs[rows, :]
            for k in (2 * pair, 2 * pair + 1):
                message(R1, k, r1, r1_next, n - 1).start()

        each(fine_residual, 2)
        hand_out(n).wait_recv()
        wot[OTHER] = wide_out[...].astype(BF)
        hand_in(n).wait_recv()
        wit[OTHER] = wide_in[...].astype(BF)
        hand_slope(n).wait_recv()

        def level_one_residual(pair, rows):
            @pl.when(n + 1 < count)
            def _():
                for k in (2 * pair, 2 * pair + 1):
                    arrived(VC, k, vc_next)

            value = vc_next[rows, :]
            value = value + 2.0 * moved(value, EVEN, rows)
            r2[rows, :] = value + 2.0 * moved(value, OTHER, rows)

            @pl.when(chip_odd)
            def _():
                for k in (2 * pair, 2 * pair + 1):
                    message(R2, k, r2, r2_next, n - 2).start()

        each(level_one_residual, 2)

        @pl.when(chip_even)
        def _even_chip():
            def level_two(k, rows):
                arrived(R2, k, r2_next)
                value = r2_next[rows, :]
                wc[rows, :] = value + 4.0 * moved(value, OTHER, rows) + r2[rows, :]

                @pl.when(n >= 2)
                def _():
                    message(WC, k, wc, wc_next, n - 2).start()

            each(level_two)

            def level_two_residual(k, rows):
                arrived(U, k, u)
                value = u[rows, :]
                r3[rows, :] = value + 4.0 * moved(value, OTHER, rows)

                @pl.when(pair_odd)
                def _():
                    message(R3, k, r3, r3_next, n - 4).start()

            each(level_two_residual)

            @pl.when(pair_even)
            def _():
                def level_three(k, rows):
                    arrived(R3, k, r3_next)
                    value = r3_next[rows, :]
                    x[rows, :] = value + 8.0 * moved(value, OTHER, rows) + r3[rows, :]

                    @pl.when(n >= 4)
                    def _():
                        message(X, k, x, x_next, n - 4).start()

                each(level_three)

                @pl.when(n >= 2)
                def _():
                    each(lambda k, rows: message(XUP, k, x, x_up, n - 2).start())

            @pl.when(pair_odd)
            def _():
                def level_three(k, rows):
                    @pl.when(n + 4 < count)
                    def _():
                        arrived(X, k, x_next)

                    value = x_next[rows, :]
                    x[rows, :] = value + 8.0 * moved(value, OTHER, rows) + r3[rows, :]
                    message(XUP, k, x, x_up, n - 2).start()

                each(level_three)

            w[...] = wc[...] + x[...]

        @pl.when(chip_odd)
        def _odd_chip():
            def level_two(k, rows):
                @pl.when(n + 2 < count)
                def _():
                    arrived(WC, k, wc_next)

                value = wc_next[rows, :]
                u_own[rows, :] = value + 4.0 * moved(value, OTHER, rows)
                message(U, k, u_own, u, n - 2).start()

            each(level_two)

            def level_two_up(k, rows):
                @pl.when(n + 2 < count)
                def _():
                    arrived(XUP, k, x_up)

                value = wc_next[rows, :] + x_up[rows, :]
                w_next[rows, :] = value
                w[rows, :] = value + 4.0 * moved(value, OTHER, rows) + r2[rows, :]
                message(W, k, w, w_next, n - 2).start()

            each(level_two_up)

        each(lambda k, rows: message(W_DOWN, k, w, w_down, n - 1).start())

        def level_one_up(k, rows):
            @pl.when(chip_even)
            def _():
                arrived(W, k, w_next)

            value = vc_next[rows, :] + w_next[rows, :]
            e_next[rows, :] = g_next[rows, :] + value
            adj[EVEN, rows, :] = gs[rows, :] + (value + 2.0 * moved(value, EVEN, rows) + r1[rows, :])
            message(E, k, adj.at[EVEN], e_next, n - 1).start()

        each(level_one_up)
        value = e_next[...]
        nexts[ODD] = value.astype(BF)
        part = tangent(value, ODD, every)
        tang[ODD] = part
        value = value + matmul(part, wit[ODD])
        adj[ODD] = value
        nexts[EVEN] = value.astype(BF)
        tang[EVEN] = tangent(value, EVEN, every)

    sent = (
        (GUESS_IN, core_one),
        (GUESS, jnp.logical_and(core_zero, n >= 1)),
        (R1, core_one),
        (VC, jnp.logical_and(core_zero, n >= 1)),
        (R2, chip_odd),
        (WC, jnp.logical_and(chip_even, n >= 2)),
        (U, chip_odd),
        (R3, pair_odd),
        (X, jnp.logical_and(pair_even, n >= 4)),
        (XUP, jnp.logical_and(chip_even, n >= 2)),
        (W, chip_odd),
        (W_DOWN, core_one),
        (E, core_one),
    )
    for kind, done in sent:

        @pl.when(done)
        def _(kind=kind):
            each(lambda k, rows: message(kind, k, r1, r1, n).wait_send())

    @pl.when(core_zero)
    def _():
        hand_out(n).wait_send()
        hand_in(n).wait_send()
        hand_slope(n).wait_send()


def gradients(tang, act, state, nexts, adj, adj_h, gi_h, go_h, gi, go, store_sem):
    def transposed_dot(a, b):
        return lax.dot_general(a, b, (((0,), (0,)), ((), ())), preferred_element_type=F32)

    stores = [
        pltpu.make_async_copy(source, target, store_sem.at[place])
        for place, (source, target) in enumerate(
            (
                (adj, adj_h),
                (gi.at[0], gi_h.at[0]),
                (go.at[0], go_h.at[0]),
                (gi.at[1], gi_h.at[1]),
                (go.at[1], go_h.at[1]),
            )
        )
    ]
    stores[0].start()
    for layer in (0, 1):
        gi[layer] = transposed_dot(state[layer], tang[layer]).astype(BF)
        stores[1 + 2 * layer].start()
        go[layer] = transposed_dot(act[layer], nexts[layer]).astype(BF)
        stores[2 + 2 * layer].start()
    for copy in stores:
        copy.wait()


def local(w_in, w_out, checkpoint, guess, terminal, rows_per=64):
    count = lax.axis_size("depth")
    pair, width, hidden = w_in.shape
    rows = terminal.shape[0]
    chunks = rows // rows_per
    anywhere = pl.BlockSpec(memory_space=pltpu.HBM)
    inside = pl.BlockSpec(memory_space=pltpu.VMEM)
    plane = pltpu.VMEM((rows, width), F32)
    kept = pl.pallas_call(
        functools.partial(kernel, count, rows_per),
        out_shape=(
            pltpu.VMEM((pair, rows, hidden), BF),
            pltpu.VMEM((pair, rows, hidden), BF),
            pltpu.VMEM((pair, rows, width), BF),
            pltpu.VMEM((pair, rows, width), BF),
            pltpu.VMEM((pair, rows, width), F32),
        ),
        in_specs=[anywhere] * 5,
        out_specs=(inside,) * 5,
        scratch_shapes=[
            pltpu.VMEM((pair, width, hidden), BF),
            pltpu.VMEM((pair, hidden, width), BF),
            pltpu.VMEM((pair + 1, hidden, width), BF),
            pltpu.VMEM((pair + 1, width, hidden), BF),
            pltpu.VMEM((hidden, width), F32),
            pltpu.VMEM((width, hidden), F32),
            plane,
            pltpu.VMEM((pair + 1, rows, hidden), F32),
        ]
        + [plane] * 20
        + [
            pltpu.SemaphoreType.DMA((6,)),
            pltpu.SemaphoreType.DMA((3,)),
            pltpu.SemaphoreType.DMA((3,)),
            pltpu.SemaphoreType.DMA((MESSAGES, chunks)),
            pltpu.SemaphoreType.DMA((MESSAGES, chunks)),
        ],
        compiler_params=pltpu.CompilerParams(
            collective_id=0, has_side_effects=True, vmem_limit_bytes=44 << 20
        ),
        name="vcycle",
    )(*(pltpu.with_memory_space_constraint(a, pltpu.HBM) for a in (w_in, w_out, checkpoint, guess, terminal)))
    return pl.pallas_call(
        gradients,
        out_shape=(
            jax.ShapeDtypeStruct((pair, rows, width), F32),
            jax.ShapeDtypeStruct((pair, width, hidden), BF),
            jax.ShapeDtypeStruct((pair, hidden, width), BF),
        ),
        in_specs=[inside] * 5,
        out_specs=(anywhere,) * 3,
        scratch_shapes=[
            pltpu.VMEM((pair, width, hidden), BF),
            pltpu.VMEM((pair, hidden, width), BF),
            pltpu.SemaphoreType.DMA((5,)),
        ],
        compiler_params=pltpu.CompilerParams(vmem_limit_bytes=24 << 20),
        name="gradients",
    )(*kept)


def solution(mesh):
    split = P("depth", None, None)
    return jax.shard_map(
        local,
        mesh=mesh,
        in_specs=(split, split, split, split, P()),
        out_specs=(split, split, split),
        check_vma=False,
    )
```

```python
import functools

import jax
import jax.numpy as jnp
from jax import lax
from jax.experimental import pallas as pl
from jax.experimental.pallas import tpu as pltpu
from jax.sharding import PartitionSpec as P

MESH = pl.DeviceIdType.MESH
BF = jnp.bfloat16
F32 = jnp.float32

GUESS_IN, GUESS, R1, VC, R2, WC, U, R3, X, XUP, W, W_DOWN, E = range(13)
MESSAGES = 13
EVEN, ODD, OTHER = 0, 1, 2


def matmul(a, b):
    return jnp.dot(a, b, preferred_element_type=F32)


def kernel(
    count, rows_per, wi_h, wo_h, cp_h, gs_h, tm_h, tang, act, state, nexts, adj,
    wi, wo, wit, wot, wide_in, wide_out, gs, slope,
    g_next, r1, r1_next, vc, vc_next, r2, r2_next, wc, wc_next, u, u_own, r3, r3_next, x, x_next, x_up, w, w_next, w_down, e_next,
    load_sem, hand_send, hand_recv, send_sem, recv_sem,
):
    n = lax.axis_index("depth")
    core_zero = lax.rem(n, 2) == 0
    core_one = lax.rem(n, 2) == 1
    chip_even = lax.rem(n, 4) == 1
    chip_odd = lax.rem(n, 4) == 3
    pair_even = lax.rem(n, 8) == 1
    pair_odd = lax.rem(n, 8) == 5
    total = gs.shape[0]
    chunks = total // rows_per
    every = pl.ds(0, total)

    def rows_of(k, several=1):
        size = rows_per * several
        return pl.ds(pl.multiple_of(k * size, size), size)

    def message(kind, k, source, target, peer):
        rows = rows_of(k)
        return pltpu.make_async_remote_copy(
            src_ref=source.at[rows],
            dst_ref=target.at[rows],
            send_sem=send_sem.at[kind, k],
            recv_sem=recv_sem.at[kind, k],
            device_id=(peer,),
            device_id_type=MESH,
        )

    def arrived(kind, k, target):
        message(kind, k, target, target, n).wait_recv()

    def each(body, several=1):
        def step(k, carry):
            body(k, rows_of(k, several))
            return carry

        lax.fori_loop(0, chunks // several, step, 0)

    def interleaved(first, second, lag=2):
        def step(k, carry):
            @pl.when(k < chunks)
            def _():
                first(k, rows_of(k))

            @pl.when(k >= lag)
            def _():
                second(k - lag, rows_of(k - lag))

            return carry

        lax.fori_loop(0, chunks + lag, step, 0)

    def down(peer):
        return pltpu.make_async_remote_copy(
            src_ref=w,
            dst_ref=w_down,
            send_sem=send_sem.at[W_DOWN, 0],
            recv_sem=recv_sem.at[W_DOWN, 0],
            device_id=(peer,),
            device_id_type=MESH,
        )

    def settle(*sent):
        for kind, done in sent:

            @pl.when(done)
            def _(kind=kind):
                each(lambda k, rows: message(kind, k, r1, r1, n).wait_send())

    def tangent(value, layer, rows):
        return (matmul(value.astype(BF), wot[layer]) * slope[layer, rows, :]).astype(BF)

    def moved(value, layer, rows):
        return matmul(tangent(value, layer, rows), wit[layer])

    loads = [
        pltpu.make_async_copy(source, target, load_sem.at[place])
        for place, (source, target) in enumerate(
            (
                (wo_h.at[0], wo.at[0]),
                (wi_h.at[0], wi.at[0]),
                (cp_h.at[0], state.at[0]),
                (wi_h.at[1], wi.at[1]),
                (wo_h.at[1], wo.at[1]),
                (gs_h.at[0], gs),
            )
        )
    ]
    for copy in loads:
        copy.start()

    barrier = pltpu.get_barrier_semaphore()
    peers = (
        (n + 1, n + 1 < count),
        (n - 1, n >= 1),
        (n + 2, jnp.logical_and(core_one, n + 2 < count)),
        (n - 2, jnp.logical_and(core_one, n >= 2)),
        (n + 4, jnp.logical_and(chip_even, n + 4 < count)),
        (n - 4, jnp.logical_and(chip_even, n >= 4)),
    )
    for peer, there in peers:

        @pl.when(there)
        def _(peer=peer):
            pl.semaphore_signal(barrier, inc=1, device_id=(peer,), device_id_type=MESH)

    greeted = sum(jnp.where(there, 1, 0) for _, there in peers)
    pl.semaphore_wait(barrier, greeted)

    @pl.when(core_one)
    def _():
        each(lambda k, rows: message(GUESS_IN, k, gs_h.at[0], g_next, n - 1).start())

    @pl.when(jnp.logical_and(core_zero, n >= 1))
    def _():
        each(lambda k, rows: message(GUESS, k, gs_h.at[0], g_next, n - 1).start())

    def terminal_copy(k):
        rows = rows_of(k)
        return pltpu.make_async_copy(tm_h.at[rows], g_next.at[rows], recv_sem.at[GUESS, k])

    @pl.when(n == count - 1)
    def _():
        each(lambda k, rows: terminal_copy(k).start())
        vc_next[...] = jnp.zeros_like(vc_next)
        wc_next[...] = jnp.zeros_like(wc_next)
        x_up[...] = jnp.zeros_like(x_up)

    @pl.when(n == count - 3)
    def _():
        x_next[...] = jnp.zeros_like(x_next)
        r2_next[...] = jnp.zeros_like(r2_next)
        u[...] = jnp.zeros_like(u)
        w_next[...] = jnp.zeros_like(w_next)

    def handed(place, source, target, peer):
        return pltpu.make_async_remote_copy(
            src_ref=source,
            dst_ref=target,
            send_sem=hand_send.at[place],
            recv_sem=hand_recv.at[place],
            device_id=(peer,),
            device_id_type=MESH,
        )

    def hand_out(peer):
        return handed(0, wide_out, wide_out, peer)

    def hand_in(peer):
        return handed(1, wide_in, wide_in, peer)

    def hand_slope(peer):
        return handed(2, slope.at[EVEN], slope.at[OTHER], peer)

    loads[0].wait()
    wot[EVEN] = wo[EVEN].T

    @pl.when(core_zero)
    def _():
        wide_out[...] = wot[EVEN].astype(F32)
        hand_out(n + 1).start()

    loads[1].wait()
    wit[EVEN] = wi[EVEN].T

    @pl.when(core_zero)
    def _():
        wide_in[...] = wit[EVEN].astype(F32)
        hand_in(n + 1).start()

    loads[2].wait()
    h = jnp.tanh(matmul(state[EVEN], wi[EVEN]))
    act[EVEN] = h.astype(BF)
    slope[EVEN] = 1.0 - h * h

    @pl.when(core_zero)
    def _():
        hand_slope(n + 1).start()

    state[ODD] = (state[EVEN].astype(F32) + matmul(act[EVEN], wo[EVEN])).astype(BF)
    loads[3].wait()
    h = jnp.tanh(matmul(state[ODD], wi[ODD]))
    act[ODD] = h.astype(BF)
    slope[ODD] = 1.0 - h * h
    loads[4].wait()
    wot[ODD] = wo[ODD].T
    wit[ODD] = wi[ODD].T
    loads[5].wait()

    @pl.when(core_zero)
    def _core_zero():
        each(lambda k, rows: arrived(GUESS_IN, k, g_next))
        value = g_next[...]
        value = value + moved(value, ODD, every)
        value = value + moved(value, EVEN, every)
        r1[...] = value - gs[...]

        def level_one(k, rows):
            arrived(R1, k, r1_next)
            value = r1_next[rows, :]
            vc[rows, :] = value + 2.0 * moved(value, EVEN, rows) + r1[rows, :]

            @pl.when(n >= 1)
            def _():
                message(VC, k, vc, vc_next, n - 1).start()

        each(level_one)
        settle((GUESS, n >= 1), (VC, n >= 1))
        hand_out(n).wait_send()
        hand_in(n).wait_send()
        hand_slope(n).wait_send()
        down(n).wait_recv()
        adj[EVEN] = gs[...] + (vc[...] + w_down[...])

        def fine(k, rows):
            arrived(E, k, e_next)
            value = e_next[rows, :]
            nexts[ODD, rows, :] = value.astype(BF)
            part = tangent(value, ODD, rows)
            tang[ODD, rows, :] = part
            value = value + matmul(part, wit[ODD])
            adj[ODD, rows, :] = value
            nexts[EVEN, rows, :] = value.astype(BF)
            tang[EVEN, rows, :] = tangent(value, EVEN, rows)

        each(fine)

    @pl.when(core_one)
    def _core_one():
        def fine_residual(k, rows):
            @pl.when(n + 1 < count)
            def _():
                arrived(GUESS, k, g_next)

            @pl.when(n + 1 == count)
            def _():
                terminal_copy(k).wait()

            value = g_next[rows, :]
            value = value + moved(value, ODD, rows)
            value = value + moved(value, EVEN, rows)
            r1[rows, :] = value - gs[rows, :]
            message(R1, k, r1, r1_next, n - 1).start()

        each(fine_residual)
        hand_out(n).wait_recv()
        wot[OTHER] = wide_out[...].astype(BF)
        hand_in(n).wait_recv()
        wit[OTHER] = wide_in[...].astype(BF)
        hand_slope(n).wait_recv()
        passes = jnp.logical_and(chip_odd, n + 1 < count)
        hears = n + 3 < count

        def level_one_residual(k, rows):
            @pl.when(n + 1 < count)
            def _():
                arrived(VC, k, vc_next)

            value = vc_next[rows, :]
            value = value + 2.0 * moved(value, EVEN, rows)
            r2[rows, :] = value + 2.0 * moved(value, OTHER, rows)

            @pl.when(passes)
            def _():
                message(R2, k, r2, r2_next, n - 2).start()

        @pl.when(chip_even)
        def _even_chip():
            def level_two(k, rows):
                @pl.when(hears)
                def _():
                    arrived(R2, k, r2_next)

                value = r2_next[rows, :]
                wc[rows, :] = value + 4.0 * moved(value, OTHER, rows) + r2[rows, :]

                @pl.when(n >= 2)
                def _():
                    message(WC, k, wc, wc_next, n - 2).start()

            interleaved(level_one_residual, level_two)

            def level_two_residual(k, rows):
                @pl.when(hears)
                def _():
                    arrived(U, k, u)

                value = u[rows, :]
                r3[rows, :] = value + 4.0 * moved(value, OTHER, rows)

                @pl.when(pair_odd)
                def _():
                    message(R3, k, r3, r3_next, n - 4).start()

            @pl.when(pair_even)
            def _():
                def level_three(k, rows):
                    arrived(R3, k, r3_next)
                    value = r3_next[rows, :]
                    x[rows, :] = value + 8.0 * moved(value, OTHER, rows) + r3[rows, :]

                    @pl.when(n >= 4)
                    def _():
                        message(X, k, x, x_next, n - 4).start()

                interleaved(level_two_residual, level_three)

                @pl.when(n >= 2)
                def _():
                    each(lambda k, rows: message(XUP, k, x, x_up, n - 2).start())

            @pl.when(pair_odd)
            def _():
                each(level_two_residual)

                def level_three(k, rows):
                    @pl.when(n + 4 < count)
                    def _():
                        arrived(X, k, x_next)

                    value = x_next[rows, :]
                    x[rows, :] = value + 8.0 * moved(value, OTHER, rows) + r3[rows, :]
                    message(XUP, k, x, x_up, n - 2).start()

                each(level_three)

            w[...] = wc[...] + x[...]

        @pl.when(chip_odd)
        def _odd_chip():
            each(level_one_residual)

            def level_two(k, rows):
                @pl.when(n + 1 < count)
                def _():
                    arrived(WC, k, wc_next)

                value = wc_next[rows, :]
                u_own[rows, :] = value + 4.0 * moved(value, OTHER, rows)

                @pl.when(passes)
                def _():
                    message(U, k, u_own, u, n - 2).start()

            each(level_two)

            def level_two_up(k, rows):
                @pl.when(n + 1 < count)
                def _():
                    arrived(XUP, k, x_up)

                value = wc_next[rows, :] + x_up[rows, :]
                w_next[rows, :] = value
                w[rows, :] = value + 4.0 * moved(value, OTHER, rows) + r2[rows, :]

                @pl.when(passes)
                def _():
                    message(W, k, w, w_next, n - 2).start()

            each(level_two_up)

        down(n - 1).start()
        settle(
            (GUESS_IN, core_one),
            (R1, core_one),
            (R2, passes),
            (WC, jnp.logical_and(chip_even, n >= 2)),
            (U, passes),
            (R3, pair_odd),
            (X, jnp.logical_and(pair_even, n >= 4)),
        )

        def level_one_up(k, rows):
            @pl.when(jnp.logical_and(chip_even, hears))
            def _():
                arrived(W, k, w_next)

            value = vc_next[rows, :] + w_next[rows, :]
            e_next[rows, :] = g_next[rows, :] + value
            adj[EVEN, rows, :] = gs[rows, :] + (value + 2.0 * moved(value, EVEN, rows) + r1[rows, :])
            message(E, k, adj.at[EVEN], e_next, n - 1).start()

        each(level_one_up)
        value = e_next[...]
        nexts[ODD] = value.astype(BF)
        part = tangent(value, ODD, every)
        tang[ODD] = part
        value = value + matmul(part, wit[ODD])
        adj[ODD] = value
        nexts[EVEN] = value.astype(BF)
        tang[EVEN] = tangent(value, EVEN, every)
        settle((XUP, jnp.logical_and(chip_even, n >= 2)), (W, passes), (E, core_one))
        down(n).wait_send()


def gradients(tang, act, state, nexts, adj, adj_h, gi_h, go_h, gi, go, store_sem):
    def transposed_dot(a, b):
        return lax.dot_general(a, b, (((0,), (0,)), ((), ())), preferred_element_type=F32)

    stores = [
        pltpu.make_async_copy(source, target, store_sem.at[place])
        for place, (source, target) in enumerate(
            (
                (adj, adj_h),
                (gi.at[0], gi_h.at[0]),
                (go.at[0], go_h.at[0]),
                (gi.at[1], gi_h.at[1]),
                (go.at[1], go_h.at[1]),
            )
        )
    ]
    stores[0].start()
    for layer in (0, 1):
        gi[layer] = transposed_dot(state[layer], tang[layer]).astype(BF)
        stores[1 + 2 * layer].start()
        go[layer] = transposed_dot(act[layer], nexts[layer]).astype(BF)
        stores[2 + 2 * layer].start()
    for copy in stores:
        copy.wait()


def local(w_in, w_out, checkpoint, guess, terminal, rows_per=64):
    count = lax.axis_size("depth")
    pair, width, hidden = w_in.shape
    rows = terminal.shape[0]
    chunks = rows // rows_per
    anywhere = pl.BlockSpec(memory_space=pltpu.HBM)
    inside = pl.BlockSpec(memory_space=pltpu.VMEM)
    plane = pltpu.VMEM((rows, width), F32)
    kept = pl.pallas_call(
        functools.partial(kernel, count, rows_per),
        out_shape=(
            pltpu.VMEM((pair, rows, hidden), BF),
            pltpu.VMEM((pair, rows, hidden), BF),
            pltpu.VMEM((pair, rows, width), BF),
            pltpu.VMEM((pair, rows, width), BF),
            pltpu.VMEM((pair, rows, width), F32),
        ),
        in_specs=[anywhere] * 5,
        out_specs=(inside,) * 5,
        scratch_shapes=[
            pltpu.VMEM((pair, width, hidden), BF),
            pltpu.VMEM((pair, hidden, width), BF),
            pltpu.VMEM((pair + 1, hidden, width), BF),
            pltpu.VMEM((pair + 1, width, hidden), BF),
            pltpu.VMEM((hidden, width), F32),
            pltpu.VMEM((width, hidden), F32),
            plane,
            pltpu.VMEM((pair + 1, rows, hidden), F32),
        ]
        + [plane] * 20
        + [
            pltpu.SemaphoreType.DMA((6,)),
            pltpu.SemaphoreType.DMA((3,)),
            pltpu.SemaphoreType.DMA((3,)),
            pltpu.SemaphoreType.DMA((MESSAGES, chunks)),
            pltpu.SemaphoreType.DMA((MESSAGES, chunks)),
        ],
        compiler_params=pltpu.CompilerParams(
            collective_id=0, has_side_effects=True, vmem_limit_bytes=44 << 20
        ),
        name="vcycle",
    )(*(pltpu.with_memory_space_constraint(a, pltpu.HBM) for a in (w_in, w_out, checkpoint, guess, terminal)))
    return pl.pallas_call(
        gradients,
        out_shape=(
            jax.ShapeDtypeStruct((pair, rows, width), F32),
            jax.ShapeDtypeStruct((pair, width, hidden), BF),
            jax.ShapeDtypeStruct((pair, hidden, width), BF),
        ),
        in_specs=[inside] * 5,
        out_specs=(anywhere,) * 3,
        scratch_shapes=[
            pltpu.VMEM((pair, width, hidden), BF),
            pltpu.VMEM((pair, hidden, width), BF),
            pltpu.SemaphoreType.DMA((5,)),
        ],
        compiler_params=pltpu.CompilerParams(vmem_limit_bytes=24 << 20),
        name="gradients",
    )(*kept)


def solution(mesh):
    split = P("depth", None, None)
    return jax.shard_map(
        local,
        mesh=mesh,
        in_specs=(split, split, split, split, P()),
        out_specs=(split, split, split),
        check_vma=False,
    )
```

```python
import functools

import jax
import jax.numpy as jnp
from jax import lax
from jax.experimental import pallas as pl
from jax.experimental.pallas import tpu as pltpu
from jax.sharding import PartitionSpec as P

MESH = pl.DeviceIdType.MESH
BF = jnp.bfloat16
F32 = jnp.float32

GUESS_IN, GUESS, R1, VC, R2, WC, U, R3, X, XUP, X_BACK, W, W_DOWN, E = range(14)
MESSAGES = 14
FEW, MANY = 4, 8
PIECES = {kind: MANY if kind in (R2, WC, U, R3, X, XUP, X_BACK, W) else FEW for kind in range(MESSAGES)}
LAG_TWO, LAG_THREE = 1, 2
EVEN, ODD, OTHER = 0, 1, 2


def matmul(a, b):
    return jnp.dot(a, b, preferred_element_type=F32)


def kernel(
    count, wi_h, wo_h, cp_h, gs_h, tm_h, tang, act, state, nexts, adj,
    wi, wo, wit, wot, wide_in, wide_out, gs, slope,
    g_next, r1, r1_next, vc, vc_next, r2, r2_next, wc, wc_next, u, u_own, r3, r3_next, x, x_next, x_up, w, w_next, w_down, e_next,
    load_sem, hand_send, hand_recv, send_sem, recv_sem,
):
    n = lax.axis_index("depth")
    core_zero = lax.rem(n, 2) == 0
    core_one = lax.rem(n, 2) == 1
    chip_even = lax.rem(n, 4) == 1
    chip_odd = lax.rem(n, 4) == 3
    pair_even = lax.rem(n, 8) == 1
    pair_odd = lax.rem(n, 8) == 5
    total = gs.shape[0]
    every = pl.ds(0, total)

    def rows_of(k, pieces):
        size = total // pieces
        return pl.ds(pl.multiple_of(k * size, size), size)

    def message(kind, k, source, target, peer, receives=None):
        rows = rows_of(k, PIECES[kind])
        return pltpu.make_async_remote_copy(
            src_ref=source.at[rows],
            dst_ref=target.at[rows],
            send_sem=send_sem.at[kind, k],
            recv_sem=recv_sem.at[kind if receives is None else receives, k],
            device_id=(peer,),
            device_id_type=MESH,
        )

    def send(kind, k, pieces, source, target, peer, receives=None):
        each_has = PIECES[kind] // pieces
        for i in range(each_has):
            message(kind, k * each_has + i, source, target, peer, receives).start()

    def arrived(kind, k, pieces, target):
        each_has = PIECES[kind] // pieces
        for i in range(each_has):
            message(kind, k * each_has + i, target, target, n).wait_recv()

    def each(body, pieces):
        def step(k, carry):
            body(k, rows_of(k, pieces))
            return carry

        lax.fori_loop(0, pieces, step, 0)

    def interleaved(first, few, second, many, lag):
        def step(k, carry):
            @pl.when(k < few)
            def _():
                first(k, rows_of(k, few))

            @pl.when(k >= lag)
            def _():
                for i in range(many // few):
                    place = (k - lag) * (many // few) + i
                    second(place, rows_of(place, many))

            return carry

        lax.fori_loop(0, few + lag, step, 0)

    def down(peer):
        return pltpu.make_async_remote_copy(
            src_ref=w,
            dst_ref=w_down,
            send_sem=send_sem.at[W_DOWN, 0],
            recv_sem=recv_sem.at[W_DOWN, 0],
            device_id=(peer,),
            device_id_type=MESH,
        )

    def settle(*sent):
        for kind, done in sent:

            @pl.when(done)
            def _(kind=kind):
                each(lambda k, rows: message(kind, k, r1, r1, n).wait_send(), PIECES[kind])

    def tangent(value, layer, rows):
        return (matmul(value.astype(BF), wot[layer]) * slope[layer, rows, :]).astype(BF)

    def moved(value, layer, rows):
        return matmul(tangent(value, layer, rows), wit[layer])

    loads = [
        pltpu.make_async_copy(source, target, load_sem.at[place])
        for place, (source, target) in enumerate(
            (
                (wo_h.at[0], wo.at[0]),
                (wi_h.at[0], wi.at[0]),
                (cp_h.at[0], state.at[0]),
                (wi_h.at[1], wi.at[1]),
                (wo_h.at[1], wo.at[1]),
                (gs_h.at[0], gs),
            )
        )
    ]
    for copy in loads:
        copy.start()

    barrier = pltpu.get_barrier_semaphore()
    peers = (
        (n + 1, n + 1 < count),
        (n - 1, n >= 1),
        (n + 2, jnp.logical_and(core_one, n + 2 < count)),
        (n - 2, jnp.logical_and(core_one, n >= 2)),
        (n + 4, jnp.logical_and(chip_even, n + 4 < count)),
        (n - 4, jnp.logical_and(chip_even, n >= 4)),
    )
    for peer, there in peers:

        @pl.when(there)
        def _(peer=peer):
            pl.semaphore_signal(barrier, inc=1, device_id=(peer,), device_id_type=MESH)

    greeted = sum(jnp.where(there, 1, 0) for _, there in peers)
    pl.semaphore_wait(barrier, greeted)

    @pl.when(core_one)
    def _():
        each(lambda k, rows: send(GUESS_IN, k, FEW, gs_h.at[0], g_next, n - 1), FEW)

    @pl.when(jnp.logical_and(core_zero, n >= 1))
    def _():
        each(lambda k, rows: send(GUESS, k, FEW, gs_h.at[0], g_next, n - 1), FEW)

    def terminal_copy(k):
        rows = rows_of(k, FEW)
        return pltpu.make_async_copy(tm_h.at[rows], g_next.at[rows], recv_sem.at[GUESS, k])

    @pl.when(n == count - 1)
    def _():
        each(lambda k, rows: terminal_copy(k).start(), FEW)
        vc_next[...] = jnp.zeros_like(vc_next)
        wc_next[...] = jnp.zeros_like(wc_next)
        x_up[...] = jnp.zeros_like(x_up)

    @pl.when(n == count - 3)
    def _():
        x_next[...] = jnp.zeros_like(x_next)
        r2_next[...] = jnp.zeros_like(r2_next)
        u[...] = jnp.zeros_like(u)
        w_next[...] = jnp.zeros_like(w_next)

    def handed(place, source, target, peer):
        return pltpu.make_async_remote_copy(
            src_ref=source,
            dst_ref=target,
            send_sem=hand_send.at[place],
            recv_sem=hand_recv.at[place],
            device_id=(peer,),
            device_id_type=MESH,
        )

    def hand_out(peer):
        return handed(0, wide_out, wide_out, peer)

    def hand_in(peer):
        return handed(1, wide_in, wide_in, peer)

    def hand_slope(peer):
        return handed(2, slope.at[EVEN], slope.at[OTHER], peer)

    loads[0].wait()
    wot[EVEN] = wo[EVEN].T

    @pl.when(core_zero)
    def _():
        wide_out[...] = wot[EVEN].astype(F32)
        hand_out(n + 1).start()

    loads[1].wait()
    wit[EVEN] = wi[EVEN].T

    @pl.when(core_zero)
    def _():
        wide_in[...] = wit[EVEN].astype(F32)
        hand_in(n + 1).start()

    loads[2].wait()
    h = jnp.tanh(matmul(state[EVEN], wi[EVEN]))
    act[EVEN] = h.astype(BF)
    slope[EVEN] = 1.0 - h * h

    @pl.when(core_zero)
    def _():
        hand_slope(n + 1).start()

    state[ODD] = (state[EVEN].astype(F32) + matmul(act[EVEN], wo[EVEN])).astype(BF)
    loads[3].wait()
    h = jnp.tanh(matmul(state[ODD], wi[ODD]))
    act[ODD] = h.astype(BF)
    slope[ODD] = 1.0 - h * h
    loads[4].wait()
    wot[ODD] = wo[ODD].T
    wit[ODD] = wi[ODD].T
    loads[5].wait()

    @pl.when(core_zero)
    def _core_zero():
        each(lambda k, rows: arrived(GUESS_IN, k, FEW, g_next), FEW)
        value = g_next[...]
        value = value + moved(value, ODD, every)
        value = value + moved(value, EVEN, every)
        r1[...] = value - gs[...]

        def level_one(k, rows):
            arrived(R1, k, FEW, r1_next)
            value = r1_next[rows, :]
            vc[rows, :] = value + 2.0 * moved(value, EVEN, rows) + r1[rows, :]

            @pl.when(n >= 1)
            def _():
                send(VC, k, FEW, vc, vc_next, n - 1)

        each(level_one, FEW)
        settle((GUESS, n >= 1), (VC, n >= 1))
        hand_out(n).wait_send()
        hand_in(n).wait_send()
        hand_slope(n).wait_send()
        down(n).wait_recv()
        adj[EVEN] = gs[...] + (vc[...] + w_down[...])

        def fine(k, rows):
            arrived(E, k, FEW, e_next)
            value = e_next[rows, :]
            nexts[ODD, rows, :] = value.astype(BF)
            part = tangent(value, ODD, rows)
            tang[ODD, rows, :] = part
            value = value + matmul(part, wit[ODD])
            adj[ODD, rows, :] = value
            nexts[EVEN, rows, :] = value.astype(BF)
            tang[EVEN, rows, :] = tangent(value, EVEN, rows)

        each(fine, FEW)

    @pl.when(core_one)
    def _core_one():
        def fine_residual(k, rows):
            @pl.when(n + 1 < count)
            def _():
                arrived(GUESS, k, FEW, g_next)

            @pl.when(n + 1 == count)
            def _():
                terminal_copy(k).wait()

            value = g_next[rows, :]
            value = value + moved(value, ODD, rows)
            value = value + moved(value, EVEN, rows)
            r1[rows, :] = value - gs[rows, :]
            send(R1, k, FEW, r1, r1_next, n - 1)

        each(fine_residual, FEW)
        hand_out(n).wait_recv()
        wot[OTHER] = wide_out[...].astype(BF)
        hand_in(n).wait_recv()
        wit[OTHER] = wide_in[...].astype(BF)
        hand_slope(n).wait_recv()
        passes = jnp.logical_and(chip_odd, n + 1 < count)
        hears = n + 3 < count

        def level_one_residual(k, rows):
            @pl.when(n + 1 < count)
            def _():
                arrived(VC, k, FEW, vc_next)

            value = vc_next[rows, :]
            value = value + 2.0 * moved(value, EVEN, rows)
            r2[rows, :] = value + 2.0 * moved(value, OTHER, rows)

            @pl.when(passes)
            def _():
                send(R2, k, FEW, r2, r2_next, n - 2)

        @pl.when(chip_even)
        def _even_chip():
            def level_two(k, rows):
                @pl.when(hears)
                def _():
                    arrived(R2, k, MANY, r2_next)

                value = r2_next[rows, :]
                wc[rows, :] = value + 4.0 * moved(value, OTHER, rows) + r2[rows, :]

                @pl.when(n >= 2)
                def _():
                    send(WC, k, MANY, wc, wc_next, n - 2)

            interleaved(level_one_residual, FEW, level_two, MANY, LAG_TWO)

            def level_two_residual(k, rows):
                @pl.when(hears)
                def _():
                    arrived(U, k, MANY, u)

                value = u[rows, :]
                r3[rows, :] = value + 4.0 * moved(value, OTHER, rows)

                @pl.when(pair_odd)
                def _():
                    send(R3, k, MANY, r3, r3_next, n - 4)

            @pl.when(pair_even)
            def _():
                def level_three(k, rows):
                    arrived(R3, k, MANY, r3_next)
                    value = r3_next[rows, :]
                    x[rows, :] = value + 8.0 * moved(value, OTHER, rows) + r3[rows, :]

                    @pl.when(n >= 4)
                    def _():
                        send(X, k, MANY, x, x_next, n - 4)

                interleaved(level_two_residual, MANY, level_three, MANY, LAG_THREE)

            @pl.when(pair_odd)
            def _():
                each(level_two_residual, MANY)

                def level_three(k, rows):
                    @pl.when(n + 4 < count)
                    def _():
                        arrived(X, k, MANY, x_next)
                        send(X_BACK, k, MANY, x_next, x_up, n + 2, XUP)

                    value = x_next[rows, :]
                    x[rows, :] = value + 8.0 * moved(value, OTHER, rows) + r3[rows, :]
                    send(XUP, k, MANY, x, x_up, n - 2)

                each(level_three, MANY)

            w[...] = wc[...] + x[...]

        @pl.when(chip_odd)
        def _odd_chip():
            each(level_one_residual, FEW)

            def level_two(k, rows):
                @pl.when(n + 1 < count)
                def _():
                    arrived(WC, k, MANY, wc_next)

                value = wc_next[rows, :]
                u_own[rows, :] = value + 4.0 * moved(value, OTHER, rows)

                @pl.when(passes)
                def _():
                    send(U, k, MANY, u_own, u, n - 2)

            each(level_two, MANY)

            def level_two_up(k, rows):
                @pl.when(n + 1 < count)
                def _():
                    arrived(XUP, k, MANY, x_up)

                value = wc_next[rows, :] + x_up[rows, :]
                w_next[rows, :] = value
                w[rows, :] = value + 4.0 * moved(value, OTHER, rows) + r2[rows, :]

                @pl.when(passes)
                def _():
                    send(W, k, MANY, w, w_next, n - 2)

            each(level_two_up, MANY)

        down(n - 1).start()
        settle(
            (GUESS_IN, core_one),
            (R1, core_one),
            (R2, passes),
            (WC, jnp.logical_and(chip_even, n >= 2)),
            (U, passes),
            (R3, pair_odd),
            (X, jnp.logical_and(pair_even, n >= 4)),
        )

        def level_one_up(k, rows):
            @pl.when(jnp.logical_and(chip_even, hears))
            def _():
                arrived(W, k, FEW, w_next)

            value = vc_next[rows, :] + w_next[rows, :]
            e_next[rows, :] = g_next[rows, :] + value
            adj[EVEN, rows, :] = gs[rows, :] + (value + 2.0 * moved(value, EVEN, rows) + r1[rows, :])
            send(E, k, FEW, adj.at[EVEN], e_next, n - 1)

        each(level_one_up, FEW)
        value = e_next[...]
        nexts[ODD] = value.astype(BF)
        part = tangent(value, ODD, every)
        tang[ODD] = part
        value = value + matmul(part, wit[ODD])
        adj[ODD] = value
        nexts[EVEN] = value.astype(BF)
        tang[EVEN] = tangent(value, EVEN, every)
        settle(
            (XUP, pair_odd),
            (X_BACK, jnp.logical_and(pair_odd, n + 4 < count)),
            (W, passes),
            (E, core_one),
        )
        down(n).wait_send()


def gradients(tang, act, state, nexts, adj, adj_h, gi_h, go_h, gi, go, store_sem):
    def transposed_dot(a, b):
        return lax.dot_general(a, b, (((0,), (0,)), ((), ())), preferred_element_type=F32)

    stores = [
        pltpu.make_async_copy(source, target, store_sem.at[place])
        for place, (source, target) in enumerate(
            (
                (adj, adj_h),
                (gi.at[0], gi_h.at[0]),
                (go.at[0], go_h.at[0]),
                (gi.at[1], gi_h.at[1]),
                (go.at[1], go_h.at[1]),
            )
        )
    ]
    stores[0].start()
    for layer in (0, 1):
        gi[layer] = transposed_dot(state[layer], tang[layer]).astype(BF)
        stores[1 + 2 * layer].start()
        go[layer] = transposed_dot(act[layer], nexts[layer]).astype(BF)
        stores[2 + 2 * layer].start()
    for copy in stores:
        copy.wait()


def local(w_in, w_out, checkpoint, guess, terminal):
    count = lax.axis_size("depth")
    pair, width, hidden = w_in.shape
    rows = terminal.shape[0]
    chunks = max(FEW, MANY)
    anywhere = pl.BlockSpec(memory_space=pltpu.HBM)
    inside = pl.BlockSpec(memory_space=pltpu.VMEM)
    plane = pltpu.VMEM((rows, width), F32)
    kept = pl.pallas_call(
        functools.partial(kernel, count),
        out_shape=(
            pltpu.VMEM((pair, rows, hidden), BF),
            pltpu.VMEM((pair, rows, hidden), BF),
            pltpu.VMEM((pair, rows, width), BF),
            pltpu.VMEM((pair, rows, width), BF),
            pltpu.VMEM((pair, rows, width), F32),
        ),
        in_specs=[anywhere] * 5,
        out_specs=(inside,) * 5,
        scratch_shapes=[
            pltpu.VMEM((pair, width, hidden), BF),
            pltpu.VMEM((pair, hidden, width), BF),
            pltpu.VMEM((pair + 1, hidden, width), BF),
            pltpu.VMEM((pair + 1, width, hidden), BF),
            pltpu.VMEM((hidden, width), F32),
            pltpu.VMEM((width, hidden), F32),
            plane,
            pltpu.VMEM((pair + 1, rows, hidden), F32),
        ]
        + [plane] * 20
        + [
            pltpu.SemaphoreType.DMA((6,)),
            pltpu.SemaphoreType.DMA((3,)),
            pltpu.SemaphoreType.DMA((3,)),
            pltpu.SemaphoreType.DMA((MESSAGES, chunks)),
            pltpu.SemaphoreType.DMA((MESSAGES, chunks)),
        ],
        compiler_params=pltpu.CompilerParams(
            collective_id=0, has_side_effects=True, vmem_limit_bytes=44 << 20
        ),
        name="vcycle",
    )(*(pltpu.with_memory_space_constraint(a, pltpu.HBM) for a in (w_in, w_out, checkpoint, guess, terminal)))
    return pl.pallas_call(
        gradients,
        out_shape=(
            jax.ShapeDtypeStruct((pair, rows, width), F32),
            jax.ShapeDtypeStruct((pair, width, hidden), BF),
            jax.ShapeDtypeStruct((pair, hidden, width), BF),
        ),
        in_specs=[inside] * 5,
        out_specs=(anywhere,) * 3,
        scratch_shapes=[
            pltpu.VMEM((pair, width, hidden), BF),
            pltpu.VMEM((pair, hidden, width), BF),
            pltpu.SemaphoreType.DMA((5,)),
        ],
        compiler_params=pltpu.CompilerParams(vmem_limit_bytes=24 << 20),
        name="gradients",
    )(*kept)


def solution(mesh):
    split = P("depth", None, None)
    return jax.shard_map(
        local,
        mesh=mesh,
        in_specs=(split, split, split, split, P()),
        out_specs=(split, split, split),
        check_vma=False,
    )
```

```python
import functools

import jax
import jax.numpy as jnp
from jax import lax
from jax.experimental import pallas as pl
from jax.experimental.pallas import tpu as pltpu
from jax.sharding import PartitionSpec as P

MESH = pl.DeviceIdType.MESH
BF = jnp.bfloat16
F32 = jnp.float32

GUESS_IN, GUESS, R1, VC, R2, WC, U, R3, X, XUP, X_BACK, W, W_DOWN, E = range(14)
MESSAGES = 14
FEW, MANY = 4, 8
PIECES = {kind: MANY if kind in (R2, WC, U, R3, X, XUP, X_BACK, W) else FEW for kind in range(MESSAGES)}
LAG_TWO = 1
EVEN, ODD, OTHER = 0, 1, 2


def matmul(a, b):
    return jnp.dot(a, b, preferred_element_type=F32)


def kernel(
    count, wi_h, wo_h, cp_h, gs_h, tm_h, tang, act, state, nexts, adj,
    wi, wo, wit, wot, wide_in, wide_out, gs, slope,
    g_next, r1, r1_next, vc, vc_next, r2, r2_next, wc, wc_next, u, u_own, r3, r3_next, x, x_next, x_up, w, w_next, w_down, e_next,
    load_sem, hand_send, hand_recv, send_sem, recv_sem,
):
    n = lax.axis_index("depth")
    core_zero = lax.rem(n, 2) == 0
    core_one = lax.rem(n, 2) == 1
    chip_even = lax.rem(n, 4) == 1
    chip_odd = lax.rem(n, 4) == 3
    pair_even = lax.rem(n, 8) == 1
    pair_odd = lax.rem(n, 8) == 5
    total = gs.shape[0]
    every = pl.ds(0, total)

    def rows_of(k, pieces):
        size = total // pieces
        return pl.ds(pl.multiple_of(k * size, size), size)

    def message(kind, k, source, target, peer, receives=None):
        rows = rows_of(k, PIECES[kind])
        return pltpu.make_async_remote_copy(
            src_ref=source.at[rows],
            dst_ref=target.at[rows],
            send_sem=send_sem.at[kind, k],
            recv_sem=recv_sem.at[kind if receives is None else receives, k],
            device_id=(peer,),
            device_id_type=MESH,
        )

    def send(kind, k, pieces, source, target, peer, receives=None):
        each_has = PIECES[kind] // pieces
        for i in range(each_has):
            message(kind, k * each_has + i, source, target, peer, receives).start()

    def arrived(kind, k, pieces, target):
        each_has = PIECES[kind] // pieces
        for i in range(each_has):
            message(kind, k * each_has + i, target, target, n).wait_recv()

    def each(body, pieces):
        def step(k, carry):
            body(k, rows_of(k, pieces))
            return carry

        lax.fori_loop(0, pieces, step, 0)

    def interleaved(first, few, second, many, lag):
        def step(k, carry):
            @pl.when(k < few)
            def _():
                first(k, rows_of(k, few))

            @pl.when(k >= lag)
            def _():
                for i in range(many // few):
                    place = (k - lag) * (many // few) + i
                    second(place, rows_of(place, many))

            return carry

        lax.fori_loop(0, few + lag, step, 0)

    def down(peer):
        return pltpu.make_async_remote_copy(
            src_ref=w,
            dst_ref=w_down,
            send_sem=send_sem.at[W_DOWN, 0],
            recv_sem=recv_sem.at[W_DOWN, 0],
            device_id=(peer,),
            device_id_type=MESH,
        )

    def settle(*sent):
        for kind, done in sent:

            @pl.when(done)
            def _(kind=kind):
                each(lambda k, rows: message(kind, k, r1, r1, n).wait_send(), PIECES[kind])

    def tangent(value, layer, rows):
        return (matmul(value.astype(BF), wot[layer]) * slope[layer, rows, :]).astype(BF)

    def moved(value, layer, rows):
        return matmul(tangent(value, layer, rows), wit[layer])

    loads = [
        pltpu.make_async_copy(source, target, load_sem.at[place])
        for place, (source, target) in enumerate(
            (
                (wo_h.at[0], wo.at[0]),
                (wi_h.at[0], wi.at[0]),
                (cp_h.at[0], state.at[0]),
                (wi_h.at[1], wi.at[1]),
                (wo_h.at[1], wo.at[1]),
                (gs_h.at[0], gs),
            )
        )
    ]
    for copy in loads:
        copy.start()

    barrier = pltpu.get_barrier_semaphore()
    peers = (
        (n + 1, n + 1 < count),
        (n - 1, n >= 1),
        (n + 2, jnp.logical_and(core_one, n + 2 < count)),
        (n - 2, jnp.logical_and(core_one, n >= 2)),
        (n + 4, jnp.logical_and(chip_even, n + 4 < count)),
        (n - 4, jnp.logical_and(chip_even, n >= 4)),
    )
    for peer, there in peers:

        @pl.when(there)
        def _(peer=peer):
            pl.semaphore_signal(barrier, inc=1, device_id=(peer,), device_id_type=MESH)

    greeted = sum(jnp.where(there, 1, 0) for _, there in peers)
    pl.semaphore_wait(barrier, greeted)

    @pl.when(core_one)
    def _():
        each(lambda k, rows: send(GUESS_IN, k, FEW, gs_h.at[0], g_next, n - 1), FEW)

    @pl.when(jnp.logical_and(core_zero, n >= 1))
    def _():
        each(lambda k, rows: send(GUESS, k, FEW, gs_h.at[0], g_next, n - 1), FEW)

    def terminal_copy(k):
        rows = rows_of(k, FEW)
        return pltpu.make_async_copy(tm_h.at[rows], g_next.at[rows], recv_sem.at[GUESS, k])

    @pl.when(n == count - 1)
    def _():
        each(lambda k, rows: terminal_copy(k).start(), FEW)
        vc_next[...] = jnp.zeros_like(vc_next)
        wc_next[...] = jnp.zeros_like(wc_next)
        x_up[...] = jnp.zeros_like(x_up)

    @pl.when(n == count - 3)
    def _():
        x_next[...] = jnp.zeros_like(x_next)
        r2_next[...] = jnp.zeros_like(r2_next)
        u[...] = jnp.zeros_like(u)
        w_next[...] = jnp.zeros_like(w_next)

    def handed(place, source, target, peer):
        return pltpu.make_async_remote_copy(
            src_ref=source,
            dst_ref=target,
            send_sem=hand_send.at[place],
            recv_sem=hand_recv.at[place],
            device_id=(peer,),
            device_id_type=MESH,
        )

    def hand_out(peer):
        return handed(0, wide_out, wide_out, peer)

    def hand_in(peer):
        return handed(1, wide_in, wide_in, peer)

    def hand_slope(peer):
        return handed(2, slope.at[EVEN], slope.at[OTHER], peer)

    loads[0].wait()
    wot[EVEN] = wo[EVEN].T

    @pl.when(core_zero)
    def _():
        wide_out[...] = wot[EVEN].astype(F32)
        hand_out(n + 1).start()

    loads[1].wait()
    wit[EVEN] = wi[EVEN].T

    @pl.when(core_zero)
    def _():
        wide_in[...] = wit[EVEN].astype(F32)
        hand_in(n + 1).start()

    loads[2].wait()
    h = jnp.tanh(matmul(state[EVEN], wi[EVEN]))
    act[EVEN] = h.astype(BF)
    slope[EVEN] = 1.0 - h * h

    @pl.when(core_zero)
    def _():
        hand_slope(n + 1).start()

    state[ODD] = (state[EVEN].astype(F32) + matmul(act[EVEN], wo[EVEN])).astype(BF)
    loads[3].wait()
    h = jnp.tanh(matmul(state[ODD], wi[ODD]))
    act[ODD] = h.astype(BF)
    slope[ODD] = 1.0 - h * h
    loads[4].wait()
    wot[ODD] = wo[ODD].T
    wit[ODD] = wi[ODD].T
    loads[5].wait()

    @pl.when(core_zero)
    def _core_zero():
        each(lambda k, rows: arrived(GUESS_IN, k, FEW, g_next), FEW)
        value = g_next[...]
        r1[...] = value + moved(value, ODD, every)

        def level_one(k, rows):
            arrived(R1, k, FEW, r1_next)
            value = r1_next[rows, :]
            fine_odd = r1[rows, :]
            vc[rows, :] = value + fine_odd - gs[rows, :] + moved(2.0 * value + fine_odd, EVEN, rows)

            @pl.when(n >= 1)
            def _():
                send(VC, k, FEW, vc, vc_next, n - 1)

        each(level_one, FEW)
        settle((GUESS, n >= 1), (VC, n >= 1))
        hand_out(n).wait_send()
        hand_in(n).wait_send()
        hand_slope(n).wait_send()
        down(n).wait_recv()
        adj[EVEN] = gs[...] + (vc[...] + w_down[...])

        def fine(k, rows):
            arrived(E, k, FEW, e_next)
            value = e_next[rows, :]
            nexts[ODD, rows, :] = value.astype(BF)
            part = tangent(value, ODD, rows)
            tang[ODD, rows, :] = part
            value = value + matmul(part, wit[ODD])
            adj[ODD, rows, :] = value
            nexts[EVEN, rows, :] = value.astype(BF)
            tang[EVEN, rows, :] = tangent(value, EVEN, rows)

        each(fine, FEW)

    @pl.when(core_one)
    def _core_one():
        def fine_residual(k, rows):
            @pl.when(n + 1 < count)
            def _():
                arrived(GUESS, k, FEW, g_next)

            @pl.when(n + 1 == count)
            def _():
                terminal_copy(k).wait()

            value = g_next[rows, :]
            value = value + moved(value, ODD, rows)
            value = value + moved(value, EVEN, rows)
            r1[rows, :] = value - gs[rows, :]
            send(R1, k, FEW, r1, r1_next, n - 1)

        each(fine_residual, FEW)
        hand_out(n).wait_recv()
        wot[OTHER] = wide_out[...].astype(BF)
        hand_in(n).wait_recv()
        wit[OTHER] = wide_in[...].astype(BF)
        hand_slope(n).wait_recv()
        passes = jnp.logical_and(chip_odd, n + 1 < count)
        hears = n + 3 < count

        def level_one_change(k, rows):
            @pl.when(n + 1 < count)
            def _():
                arrived(VC, k, FEW, vc_next)

            value = vc_next[rows, :]
            return value + 2.0 * moved(value, EVEN, rows)

        @pl.when(chip_even)
        def _even_chip():
            def level_one_residual(k, rows):
                r2[rows, :] = level_one_change(k, rows)

            def level_two(k, rows):
                @pl.when(hears)
                def _():
                    arrived(R2, k, MANY, r2_next)

                value, own = r2_next[rows, :], r2[rows, :]
                wc[rows, :] = value + own + moved(4.0 * value + 2.0 * own, OTHER, rows)

                @pl.when(n >= 2)
                def _():
                    send(WC, k, MANY, wc, wc_next, n - 2)

            interleaved(level_one_residual, FEW, level_two, MANY, LAG_TWO)

            @pl.when(pair_even)
            def _():
                def level_three(k, rows):
                    arrived(U, k, MANY, u)
                    arrived(R3, k, MANY, r3_next)
                    value, own = r3_next[rows, :], u[rows, :]
                    x[rows, :] = value + own + moved(8.0 * value + 4.0 * own, OTHER, rows)

                    @pl.when(n >= 4)
                    def _():
                        send(X, k, MANY, x, x_next, n - 4)

                each(level_three, MANY)

            @pl.when(pair_odd)
            def _():
                def level_two_residual(k, rows):
                    @pl.when(hears)
                    def _():
                        arrived(U, k, MANY, u)

                    value = u[rows, :]
                    r3[rows, :] = value + 4.0 * moved(value, OTHER, rows)
                    send(R3, k, MANY, r3, r3_next, n - 4)

                each(level_two_residual, MANY)

                def level_three(k, rows):
                    @pl.when(n + 4 < count)
                    def _():
                        arrived(X, k, MANY, x_next)
                        send(X_BACK, k, MANY, x_next, x_up, n + 2, XUP)

                    value = x_next[rows, :]
                    x[rows, :] = value + 8.0 * moved(value, OTHER, rows) + r3[rows, :]
                    send(XUP, k, MANY, x, x_up, n - 2)

                each(level_three, MANY)

            w[...] = wc[...] + x[...]

        @pl.when(chip_odd)
        def _odd_chip():
            def level_one_residual(k, rows):
                value = level_one_change(k, rows)
                r2[rows, :] = value + 2.0 * moved(value, OTHER, rows)

                @pl.when(passes)
                def _():
                    send(R2, k, FEW, r2, r2_next, n - 2)

            each(level_one_residual, FEW)

            def level_two(k, rows):
                @pl.when(n + 1 < count)
                def _():
                    arrived(WC, k, MANY, wc_next)

                value = wc_next[rows, :]
                u_own[rows, :] = value + 4.0 * moved(value, OTHER, rows)

                @pl.when(passes)
                def _():
                    send(U, k, MANY, u_own, u, n - 2)

            each(level_two, MANY)

            def level_two_up(k, rows):
                @pl.when(n + 1 < count)
                def _():
                    arrived(XUP, k, MANY, x_up)

                value = wc_next[rows, :] + x_up[rows, :]
                w_next[rows, :] = value
                w[rows, :] = value + 4.0 * moved(value, OTHER, rows) + r2[rows, :]

                @pl.when(passes)
                def _():
                    send(W, k, MANY, w, w_next, n - 2)

            each(level_two_up, MANY)

        down(n - 1).start()
        settle(
            (GUESS_IN, core_one),
            (R1, core_one),
            (R2, passes),
            (WC, jnp.logical_and(chip_even, n >= 2)),
            (U, passes),
            (R3, pair_odd),
            (X, jnp.logical_and(pair_even, n >= 4)),
        )

        def level_one_up(k, rows):
            @pl.when(jnp.logical_and(chip_even, hears))
            def _():
                arrived(W, k, FEW, w_next)

            value = vc_next[rows, :] + w_next[rows, :]
            e_next[rows, :] = g_next[rows, :] + value
            adj[EVEN, rows, :] = gs[rows, :] + (value + 2.0 * moved(value, EVEN, rows) + r1[rows, :])
            send(E, k, FEW, adj.at[EVEN], e_next, n - 1)

        each(level_one_up, FEW)
        value = e_next[...]
        nexts[ODD] = value.astype(BF)
        part = tangent(value, ODD, every)
        tang[ODD] = part
        value = value + matmul(part, wit[ODD])
        adj[ODD] = value
        nexts[EVEN] = value.astype(BF)
        tang[EVEN] = tangent(value, EVEN, every)
        settle(
            (XUP, pair_odd),
            (X_BACK, jnp.logical_and(pair_odd, n + 4 < count)),
            (W, passes),
            (E, core_one),
        )
        down(n).wait_send()


def gradients(tang, act, state, nexts, adj, adj_h, gi_h, go_h, gi, go, store_sem):
    def transposed_dot(a, b):
        return lax.dot_general(a, b, (((0,), (0,)), ((), ())), preferred_element_type=F32)

    half = go.shape[1] // 2
    stores = [
        pltpu.make_async_copy(source, target, store_sem.at[place])
        for place, (source, target) in enumerate(
            (
                (adj, adj_h),
                (gi.at[0], gi_h.at[0]),
                (go.at[0], go_h.at[0]),
                (gi.at[1], gi_h.at[1]),
                (go.at[1, pl.ds(0, half)], go_h.at[1, pl.ds(0, half)]),
                (go.at[1, pl.ds(half, half)], go_h.at[1, pl.ds(half, half)]),
            )
        )
    ]
    stores[0].start()
    gi[0] = transposed_dot(state[0], tang[0]).astype(BF)
    stores[1].start()
    go[0] = transposed_dot(act[0], nexts[0]).astype(BF)
    stores[2].start()
    gi[1] = transposed_dot(state[1], tang[1]).astype(BF)
    stores[3].start()
    for part in (0, 1):
        some = pl.ds(part * half, half)
        go[1, some, :] = transposed_dot(act[1, :, some], nexts[1]).astype(BF)
        stores[4 + part].start()
    for copy in stores:
        copy.wait()


def local(w_in, w_out, checkpoint, guess, terminal):
    count = lax.axis_size("depth")
    pair, width, hidden = w_in.shape
    rows = terminal.shape[0]
    chunks = max(FEW, MANY)
    anywhere = pl.BlockSpec(memory_space=pltpu.HBM)
    inside = pl.BlockSpec(memory_space=pltpu.VMEM)
    plane = pltpu.VMEM((rows, width), F32)
    kept = pl.pallas_call(
        functools.partial(kernel, count),
        out_shape=(
            pltpu.VMEM((pair, rows, hidden), BF),
            pltpu.VMEM((pair, rows, hidden), BF),
            pltpu.VMEM((pair, rows, width), BF),
            pltpu.VMEM((pair, rows, width), BF),
            pltpu.VMEM((pair, rows, width), F32),
        ),
        in_specs=[anywhere] * 5,
        out_specs=(inside,) * 5,
        scratch_shapes=[
            pltpu.VMEM((pair, width, hidden), BF),
            pltpu.VMEM((pair, hidden, width), BF),
            pltpu.VMEM((pair + 1, hidden, width), BF),
            pltpu.VMEM((pair + 1, width, hidden), BF),
            pltpu.VMEM((hidden, width), F32),
            pltpu.VMEM((width, hidden), F32),
            plane,
            pltpu.VMEM((pair + 1, rows, hidden), F32),
        ]
        + [plane] * 20
        + [
            pltpu.SemaphoreType.DMA((6,)),
            pltpu.SemaphoreType.DMA((3,)),
            pltpu.SemaphoreType.DMA((3,)),
            pltpu.SemaphoreType.DMA((MESSAGES, chunks)),
            pltpu.SemaphoreType.DMA((MESSAGES, chunks)),
        ],
        compiler_params=pltpu.CompilerParams(
            collective_id=0, has_side_effects=True, vmem_limit_bytes=44 << 20
        ),
        name="vcycle",
    )(*(pltpu.with_memory_space_constraint(a, pltpu.HBM) for a in (w_in, w_out, checkpoint, guess, terminal)))
    return pl.pallas_call(
        gradients,
        out_shape=(
            jax.ShapeDtypeStruct((pair, rows, width), F32),
            jax.ShapeDtypeStruct((pair, width, hidden), BF),
            jax.ShapeDtypeStruct((pair, hidden, width), BF),
        ),
        in_specs=[inside] * 5,
        out_specs=(anywhere,) * 3,
        scratch_shapes=[
            pltpu.VMEM((pair, width, hidden), BF),
            pltpu.VMEM((pair, hidden, width), BF),
            pltpu.SemaphoreType.DMA((6,)),
        ],
        compiler_params=pltpu.CompilerParams(vmem_limit_bytes=24 << 20),
        name="gradients",
    )(*kept)


def solution(mesh):
    split = P("depth", None, None)
    return jax.shard_map(
        local,
        mesh=mesh,
        in_specs=(split, split, split, split, P()),
        out_specs=(split, split, split),
        check_vma=False,
    )
```

```python
import functools

import jax
import jax.numpy as jnp
from jax import lax
from jax.experimental import pallas as pl
from jax.experimental.pallas import tpu as pltpu
from jax.sharding import PartitionSpec as P

MESH = pl.DeviceIdType.MESH
BF = jnp.bfloat16
F32 = jnp.float32

GUESS_IN, GUESS, R1, VC, R2, WC, U, R3, X, XUP, X_BACK, W, W_DOWN, E = range(14)
MESSAGES = 14
FEW, MANY = 4, 8
PIECES = {kind: MANY if kind in (R1, VC, R2, WC, U, R3, X, XUP, X_BACK, W) else FEW for kind in range(MESSAGES)}
LAG_TWO = 1
EVEN, ODD, OTHER = 0, 1, 2


def matmul(a, b):
    return jnp.dot(a, b, preferred_element_type=F32)


def kernel(
    count, wi_h, wo_h, cp_h, gs_h, tm_h, tang, act, state, nexts, adj,
    wi, wo, wit, wot, wide_in, wide_out, gs, slope,
    g_next, r1, r1_next, vc, vc_next, r2, r2_next, wc, wc_next, u, u_own, r3, r3_next, x, x_next, x_up, w, w_next, w_down, e_next,
    load_sem, hand_send, hand_recv, send_sem, recv_sem,
):
    n = lax.axis_index("depth")
    core_zero = lax.rem(n, 2) == 0
    core_one = lax.rem(n, 2) == 1
    chip_even = lax.rem(n, 4) == 1
    chip_odd = lax.rem(n, 4) == 3
    pair_even = lax.rem(n, 8) == 1
    pair_odd = lax.rem(n, 8) == 5
    total = gs.shape[0]
    every = pl.ds(0, total)

    def rows_of(k, pieces):
        size = total // pieces
        return pl.ds(pl.multiple_of(k * size, size), size)

    def message(kind, k, source, target, peer, receives=None):
        rows = rows_of(k, PIECES[kind])
        return pltpu.make_async_remote_copy(
            src_ref=source.at[rows],
            dst_ref=target.at[rows],
            send_sem=send_sem.at[kind, k],
            recv_sem=recv_sem.at[kind if receives is None else receives, k],
            device_id=(peer,),
            device_id_type=MESH,
        )

    def send(kind, k, pieces, source, target, peer, receives=None):
        each_has = PIECES[kind] // pieces
        for i in range(each_has):
            message(kind, k * each_has + i, source, target, peer, receives).start()

    def arrived(kind, k, pieces, target):
        each_has = PIECES[kind] // pieces
        for i in range(each_has):
            message(kind, k * each_has + i, target, target, n).wait_recv()

    def each(body, pieces):
        def step(k, carry):
            body(k, rows_of(k, pieces))
            return carry

        lax.fori_loop(0, pieces, step, 0)

    def interleaved(first, few, second, many, lag):
        def step(k, carry):
            @pl.when(k < few)
            def _():
                first(k, rows_of(k, few))

            @pl.when(k >= lag)
            def _():
                for i in range(many // few):
                    place = (k - lag) * (many // few) + i
                    second(place, rows_of(place, many))

            return carry

        lax.fori_loop(0, few + lag, step, 0)

    def down(peer):
        return pltpu.make_async_remote_copy(
            src_ref=w,
            dst_ref=w_down,
            send_sem=send_sem.at[W_DOWN, 0],
            recv_sem=recv_sem.at[W_DOWN, 0],
            device_id=(peer,),
            device_id_type=MESH,
        )

    def settle(*sent):
        for kind, done in sent:

            @pl.when(done)
            def _(kind=kind):
                each(lambda k, rows: message(kind, k, r1, r1, n).wait_send(), PIECES[kind])

    def tangent(value, layer, rows):
        return (matmul(value.astype(BF), wot[layer]) * slope[layer, rows, :]).astype(BF)

    def moved(value, layer, rows):
        return matmul(tangent(value, layer, rows), wit[layer])

    loads = [
        pltpu.make_async_copy(source, target, load_sem.at[place])
        for place, (source, target) in enumerate(
            (
                (wo_h.at[0], wo.at[0]),
                (wi_h.at[0], wi.at[0]),
                (cp_h.at[0], state.at[0]),
                (wi_h.at[1], wi.at[1]),
                (wo_h.at[1], wo.at[1]),
                (gs_h.at[0], gs),
            )
        )
    ]
    for copy in loads:
        copy.start()

    barrier = pltpu.get_barrier_semaphore()
    peers = (
        (n + 1, n + 1 < count),
        (n - 1, n >= 1),
        (n + 2, jnp.logical_and(core_one, n + 2 < count)),
        (n - 2, jnp.logical_and(core_one, n >= 2)),
        (n + 4, jnp.logical_and(chip_even, n + 4 < count)),
        (n - 4, jnp.logical_and(chip_even, n >= 4)),
    )
    for peer, there in peers:

        @pl.when(there)
        def _(peer=peer):
            pl.semaphore_signal(barrier, inc=1, device_id=(peer,), device_id_type=MESH)

    greeted = sum(jnp.where(there, 1, 0) for _, there in peers)
    pl.semaphore_wait(barrier, greeted)

    @pl.when(core_one)
    def _():
        each(lambda k, rows: send(GUESS_IN, k, FEW, gs_h.at[0], g_next, n - 1), FEW)

    @pl.when(jnp.logical_and(core_zero, n >= 1))
    def _():
        each(lambda k, rows: send(GUESS, k, FEW, gs_h.at[0], g_next, n - 1), FEW)

    def terminal_copy(k):
        rows = rows_of(k, FEW)
        return pltpu.make_async_copy(tm_h.at[rows], g_next.at[rows], recv_sem.at[GUESS, k])

    @pl.when(n == count - 1)
    def _():
        each(lambda k, rows: terminal_copy(k).start(), FEW)
        vc_next[...] = jnp.zeros_like(vc_next)
        wc_next[...] = jnp.zeros_like(wc_next)
        x_up[...] = jnp.zeros_like(x_up)

    @pl.when(n == count - 3)
    def _():
        x_next[...] = jnp.zeros_like(x_next)
        r2_next[...] = jnp.zeros_like(r2_next)
        u[...] = jnp.zeros_like(u)
        w_next[...] = jnp.zeros_like(w_next)

    def handed(place, source, target, peer):
        return pltpu.make_async_remote_copy(
            src_ref=source,
            dst_ref=target,
            send_sem=hand_send.at[place],
            recv_sem=hand_recv.at[place],
            device_id=(peer,),
            device_id_type=MESH,
        )

    def hand_out(peer):
        return handed(0, wide_out, wide_out, peer)

    def hand_in(peer):
        return handed(1, wide_in, wide_in, peer)

    def hand_slope(peer):
        return handed(2, slope.at[EVEN], slope.at[OTHER], peer)

    loads[0].wait()
    wot[EVEN] = wo[EVEN].T

    @pl.when(core_zero)
    def _():
        wide_out[...] = wot[EVEN].astype(F32)
        hand_out(n + 1).start()

    loads[1].wait()
    wit[EVEN] = wi[EVEN].T

    @pl.when(core_zero)
    def _():
        wide_in[...] = wit[EVEN].astype(F32)
        hand_in(n + 1).start()

    loads[2].wait()
    h = jnp.tanh(matmul(state[EVEN], wi[EVEN]))
    act[EVEN] = h.astype(BF)
    slope[EVEN] = 1.0 - h * h

    @pl.when(core_zero)
    def _():
        hand_slope(n + 1).start()

    state[ODD] = (state[EVEN].astype(F32) + matmul(act[EVEN], wo[EVEN])).astype(BF)
    loads[3].wait()
    h = jnp.tanh(matmul(state[ODD], wi[ODD]))
    act[ODD] = h.astype(BF)
    slope[ODD] = 1.0 - h * h
    loads[4].wait()
    wot[ODD] = wo[ODD].T
    wit[ODD] = wi[ODD].T
    loads[5].wait()

    @pl.when(core_zero)
    def _core_zero():
        each(lambda k, rows: arrived(GUESS_IN, k, FEW, g_next), FEW)
        value = g_next[...]
        r1[...] = value + moved(value, ODD, every)

        def level_one(k, rows):
            arrived(R1, k, MANY, r1_next)
            value = r1_next[rows, :]
            fine_odd = r1[rows, :]
            vc[rows, :] = value + fine_odd - gs[rows, :] + moved(2.0 * value + fine_odd, EVEN, rows)

            @pl.when(n >= 1)
            def _():
                send(VC, k, MANY, vc, vc_next, n - 1)

        each(level_one, MANY)
        settle((GUESS, n >= 1), (VC, n >= 1))
        hand_out(n).wait_send()
        hand_in(n).wait_send()
        hand_slope(n).wait_send()
        down(n).wait_recv()
        adj[EVEN] = gs[...] + (vc[...] + w_down[...])

        def fine(k, rows):
            arrived(E, k, FEW, e_next)
            value = e_next[rows, :]
            nexts[ODD, rows, :] = value.astype(BF)
            part = tangent(value, ODD, rows)
            tang[ODD, rows, :] = part
            value = value + matmul(part, wit[ODD])
            adj[ODD, rows, :] = value
            nexts[EVEN, rows, :] = value.astype(BF)
            tang[EVEN, rows, :] = tangent(value, EVEN, rows)

        each(fine, FEW)

    @pl.when(core_one)
    def _core_one():
        def fine_residual(k, rows):
            @pl.when(n + 1 < count)
            def _():
                arrived(GUESS, k, FEW, g_next)

            @pl.when(n + 1 == count)
            def _():
                terminal_copy(k).wait()

            value = g_next[rows, :]
            value = value + moved(value, ODD, rows)
            value = value + moved(value, EVEN, rows)
            r1[rows, :] = value - gs[rows, :]
            send(R1, k, FEW, r1, r1_next, n - 1)

        each(fine_residual, FEW)
        hand_out(n).wait_recv()
        wot[OTHER] = wide_out[...].astype(BF)
        hand_in(n).wait_recv()
        wit[OTHER] = wide_in[...].astype(BF)
        hand_slope(n).wait_recv()
        passes = jnp.logical_and(chip_odd, n + 1 < count)
        hears = n + 3 < count

        def level_one_change(k, rows):
            @pl.when(n + 1 < count)
            def _():
                arrived(VC, k, FEW, vc_next)

            value = vc_next[rows, :]
            return value + 2.0 * moved(value, EVEN, rows)

        @pl.when(chip_even)
        def _even_chip():
            def level_one_residual(k, rows):
                r2[rows, :] = level_one_change(k, rows)

            def level_two(k, rows):
                @pl.when(hears)
                def _():
                    arrived(R2, k, MANY, r2_next)

                value, own = r2_next[rows, :], r2[rows, :]
                wc[rows, :] = value + own + moved(4.0 * value + 2.0 * own, OTHER, rows)

                @pl.when(n >= 2)
                def _():
                    send(WC, k, MANY, wc, wc_next, n - 2)

            interleaved(level_one_residual, FEW, level_two, MANY, LAG_TWO)

            @pl.when(pair_even)
            def _():
                def level_three(k, rows):
                    arrived(U, k, MANY, u)
                    arrived(R3, k, MANY, r3_next)
                    value, own = r3_next[rows, :], u[rows, :]
                    x[rows, :] = value + own + moved(8.0 * value + 4.0 * own, OTHER, rows)

                    @pl.when(n >= 4)
                    def _():
                        send(X, k, MANY, x, x_next, n - 4)

                each(level_three, MANY)

            @pl.when(pair_odd)
            def _():
                def level_two_residual(k, rows):
                    @pl.when(hears)
                    def _():
                        arrived(U, k, MANY, u)

                    value = u[rows, :]
                    r3[rows, :] = value + 4.0 * moved(value, OTHER, rows)
                    send(R3, k, MANY, r3, r3_next, n - 4)

                each(level_two_residual, MANY)

                def level_three(k, rows):
                    @pl.when(n + 4 < count)
                    def _():
                        arrived(X, k, MANY, x_next)
                        send(X_BACK, k, MANY, x_next, x_up, n + 2, XUP)

                    value = x_next[rows, :]
                    x[rows, :] = value + 8.0 * moved(value, OTHER, rows) + r3[rows, :]
                    send(XUP, k, MANY, x, x_up, n - 2)

                each(level_three, MANY)

            w[...] = wc[...] + x[...]

        @pl.when(chip_odd)
        def _odd_chip():
            def level_one_residual(k, rows):
                value = level_one_change(k, rows)
                r2[rows, :] = value + 2.0 * moved(value, OTHER, rows)

                @pl.when(passes)
                def _():
                    send(R2, k, FEW, r2, r2_next, n - 2)

            each(level_one_residual, FEW)

            def level_two(k, rows):
                @pl.when(n + 1 < count)
                def _():
                    arrived(WC, k, MANY, wc_next)

                value = wc_next[rows, :]
                u_own[rows, :] = value + 4.0 * moved(value, OTHER, rows)

                @pl.when(passes)
                def _():
                    send(U, k, MANY, u_own, u, n - 2)

            each(level_two, MANY)

            def level_two_up(k, rows):
                @pl.when(n + 1 < count)
                def _():
                    arrived(XUP, k, MANY, x_up)

                value = wc_next[rows, :] + x_up[rows, :]
                w_next[rows, :] = value
                w[rows, :] = value + 4.0 * moved(value, OTHER, rows) + r2[rows, :]

                @pl.when(passes)
                def _():
                    send(W, k, MANY, w, w_next, n - 2)

            each(level_two_up, MANY)

        down(n - 1).start()
        settle(
            (GUESS_IN, core_one),
            (R1, core_one),
            (R2, passes),
            (WC, jnp.logical_and(chip_even, n >= 2)),
            (U, passes),
            (R3, pair_odd),
            (X, jnp.logical_and(pair_even, n >= 4)),
        )

        def level_one_up(k, rows):
            @pl.when(jnp.logical_and(chip_even, hears))
            def _():
                arrived(W, k, FEW, w_next)

            value = vc_next[rows, :] + w_next[rows, :]
            e_next[rows, :] = g_next[rows, :] + value
            adj[EVEN, rows, :] = gs[rows, :] + (value + 2.0 * moved(value, EVEN, rows) + r1[rows, :])
            send(E, k, FEW, adj.at[EVEN], e_next, n - 1)

        each(level_one_up, FEW)
        value = e_next[...]
        nexts[ODD] = value.astype(BF)
        part = tangent(value, ODD, every)
        tang[ODD] = part
        value = value + matmul(part, wit[ODD])
        adj[ODD] = value
        nexts[EVEN] = value.astype(BF)
        tang[EVEN] = tangent(value, EVEN, every)
        settle(
            (XUP, pair_odd),
            (X_BACK, jnp.logical_and(pair_odd, n + 4 < count)),
            (W, passes),
            (E, core_one),
        )
        down(n).wait_send()


def gradients(tang, act, state, nexts, adj, adj_h, gi_h, go_h, gi, go, store_sem):
    def transposed_dot(a, b):
        return lax.dot_general(a, b, (((0,), (0,)), ((), ())), preferred_element_type=F32)

    half = go.shape[1] // 2
    stores = [
        pltpu.make_async_copy(source, target, store_sem.at[place])
        for place, (source, target) in enumerate(
            (
                (adj, adj_h),
                (gi.at[0], gi_h.at[0]),
                (go.at[0], go_h.at[0]),
                (gi.at[1], gi_h.at[1]),
                (go.at[1, pl.ds(0, half)], go_h.at[1, pl.ds(0, half)]),
                (go.at[1, pl.ds(half, half)], go_h.at[1, pl.ds(half, half)]),
            )
        )
    ]
    stores[0].start()
    gi[0] = transposed_dot(state[0], tang[0]).astype(BF)
    stores[1].start()
    go[0] = transposed_dot(act[0], nexts[0]).astype(BF)
    stores[2].start()
    gi[1] = transposed_dot(state[1], tang[1]).astype(BF)
    stores[3].start()
    for part in (0, 1):
        some = pl.ds(part * half, half)
        go[1, some, :] = transposed_dot(act[1, :, some], nexts[1]).astype(BF)
        stores[4 + part].start()
    for copy in stores:
        copy.wait()


def local(w_in, w_out, checkpoint, guess, terminal):
    count = lax.axis_size("depth")
    pair, width, hidden = w_in.shape
    rows = terminal.shape[0]
    chunks = max(FEW, MANY)
    anywhere = pl.BlockSpec(memory_space=pltpu.HBM)
    inside = pl.BlockSpec(memory_space=pltpu.VMEM)
    plane = pltpu.VMEM((rows, width), F32)
    kept = pl.pallas_call(
        functools.partial(kernel, count),
        out_shape=(
            pltpu.VMEM((pair, rows, hidden), BF),
            pltpu.VMEM((pair, rows, hidden), BF),
            pltpu.VMEM((pair, rows, width), BF),
            pltpu.VMEM((pair, rows, width), BF),
            pltpu.VMEM((pair, rows, width), F32),
        ),
        in_specs=[anywhere] * 5,
        out_specs=(inside,) * 5,
        scratch_shapes=[
            pltpu.VMEM((pair, width, hidden), BF),
            pltpu.VMEM((pair, hidden, width), BF),
            pltpu.VMEM((pair + 1, hidden, width), BF),
            pltpu.VMEM((pair + 1, width, hidden), BF),
            pltpu.VMEM((hidden, width), F32),
            pltpu.VMEM((width, hidden), F32),
            plane,
            pltpu.VMEM((pair + 1, rows, hidden), F32),
        ]
        + [plane] * 20
        + [
            pltpu.SemaphoreType.DMA((6,)),
            pltpu.SemaphoreType.DMA((3,)),
            pltpu.SemaphoreType.DMA((3,)),
            pltpu.SemaphoreType.DMA((MESSAGES, chunks)),
            pltpu.SemaphoreType.DMA((MESSAGES, chunks)),
        ],
        compiler_params=pltpu.CompilerParams(
            collective_id=0, has_side_effects=True, vmem_limit_bytes=44 << 20
        ),
        name="vcycle",
    )(*(pltpu.with_memory_space_constraint(a, pltpu.HBM) for a in (w_in, w_out, checkpoint, guess, terminal)))
    return pl.pallas_call(
        gradients,
        out_shape=(
            jax.ShapeDtypeStruct((pair, rows, width), F32),
            jax.ShapeDtypeStruct((pair, width, hidden), BF),
            jax.ShapeDtypeStruct((pair, hidden, width), BF),
        ),
        in_specs=[inside] * 5,
        out_specs=(anywhere,) * 3,
        scratch_shapes=[
            pltpu.VMEM((pair, width, hidden), BF),
            pltpu.VMEM((pair, hidden, width), BF),
            pltpu.SemaphoreType.DMA((6,)),
        ],
        compiler_params=pltpu.CompilerParams(vmem_limit_bytes=24 << 20),
        name="gradients",
    )(*kept)


def solution(mesh):
    split = P("depth", None, None)
    return jax.shard_map(
        local,
        mesh=mesh,
        in_specs=(split, split, split, split, P()),
        out_specs=(split, split, split),
        check_vma=False,
    )
```
